32 devices in a mesh: groups: 2 (over x), dap: 16 (over z, y, core).
Axes of the slice: x: 2, y: 2, z: 4, core: 2. Of those that a mesh axis runs over, the one named last changes fastest.
Arguments:
- homolog_tensor: bfloat16 [128, 32, 256], P(('groups', 'dap')), parts along dimension 0, may hold values from -1 to 1
- couple_tensor: bfloat16 [64, 32, 128], P(('groups', 'dap')), parts along dimension 0, may hold values from -6 to 6
- horizontal_drop_filter: int32 [64, 256], P('groups'), parts along dimension 0, may hold values 0 or 1
- couple_offset_matrix: bfloat16 [128, 8], replicated, may hold values from -0.29882812 to 0.29882812
- horizontal_attend_matrix: bfloat16 [256, 1024], replicated, may hold values from -0.375 to 0.375
- horizontal_exit_matrix: bfloat16 [256, 256], replicated, may hold values from -0.375 to 0.375
- vertical_attend_matrix: bfloat16 [256, 1024], replicated, may hold values from -0.375 to 0.375
- vertical_exit_matrix: bfloat16 [256, 256], replicated, may hold values from -0.375 to 0.375
- averaged_product_flanks: bfloat16 [256, 64], replicated, may hold values from -0.375 to 0.375
- averaged_product_exit: bfloat16 [1024, 128], replicated, may hold values from -1 to 1
Outputs:
- alignment_output: bfloat16 [128, 32, 256], P('groups', 'dap'), parts along dimension 0
- pair_output_state: bfloat16 [64, 32, 128], P(('groups', 'dap')), parts along dimension 0
The draws below stay inside these ranges and needn't reach their ends.
There are 2 independent parts, one for each index of `groups`. The reference program is written for one: setup_inputs(seed, part) draws one part's arguments, and reference() takes and returns one part's arrays. A program takes and returns all parts, laid end to end along the dimension named above; an argument that names none is the same for every part. Nothing has to cross between parts.
All inputs are finite; a program needn't handle non-finite values.
Results may differ from the reference program's by a relative error of at most 0.012.
Values may be sent and summed in bfloat16 or wider, within the bound.
No kernel may reach another device: no remote copies, remote signals or barrier semaphores. Data moves between devices by JAX's collectives and lax.ppermute only.
A program may use at most 64 MiB of HBM per device.

```python
import jax
import jax.numpy as jnp
from jax import lax

FEATURE_SIZE = 256
CZ = 128
HEAD_NUMBER = 8
HEAD_WIDTH = 32
FACTOR_FEATURES = 32
HOMOLOG_TOTAL = 64
AMINO_TOTAL = 32


def set_ends(result, stream_key, least, largest):
    longest = result.shape.index(max(result.shape))
    spots = []
    for shift in (0, 1):
        where = [jax.random.randint(jax.random.fold_in(stream_key, axis), (), 0, length) for axis, length in enumerate(result.shape)]
        where[longest] = (where[longest] + shift) % result.shape[longest]
        spots.append(tuple(where))
    return result.at[spots[0]].set(least).at[spots[1]].set(largest)


def level_of(rng, shape, cuts, least, largest):
    def one(position, parts):
        draws = jax.random.uniform(jax.random.fold_in(jax.random.fold_in(rng, 6), position), (parts,), jnp.float32, least / len(cuts), largest / len(cuts))
        return jnp.repeat(jnp.exp(draws), shape[position] // parts).reshape((-1,) + (1,) * (len(shape) - position - 1))

    factor_of = one(*cuts[0])
    for cut in cuts[1:]:
        factor_of = factor_of * one(*cut)
    return factor_of


def gaussian(own_key, shape, width, reach, split=(), kind=jnp.bfloat16):
    factor_of = level_of(own_key, shape, split, -0.22, 0.18) if split else 1.0
    result = jax.random.normal(own_key, shape, jnp.float32) * width * factor_of
    return jnp.minimum(jnp.maximum(result, -reach), reach).astype(kind)


def setup_inputs(seed: int = 0, part: int = 0) -> dict:
    splits = jax.random.split(jax.random.key(seed), 11)
    part_keys = jax.random.split(jax.random.fold_in(splits[10], part), 11)
    return {
        "homolog_tensor": gaussian(part_keys[0], (HOMOLOG_TOTAL, AMINO_TOTAL, FEATURE_SIZE), 0.2, 1.0, ((0, 16),)),
        "couple_tensor": gaussian(part_keys[1], (AMINO_TOTAL, AMINO_TOTAL, CZ), 1.0, 6.0, ((0, 16),)),
        "horizontal_drop_filter": set_ends((jax.random.randint(part_keys[2], (AMINO_TOTAL, FEATURE_SIZE), 0, 10) < 9).astype(jnp.int32), jax.random.fold_in(part_keys[2], 1), 0, 1),
        "couple_offset_matrix": gaussian(splits[3], (CZ, HEAD_NUMBER), 0.1, 0.29882812),
        "horizontal_attend_matrix": gaussian(splits[4], (FEATURE_SIZE, 4 * HEAD_NUMBER * HEAD_WIDTH), FEATURE_SIZE ** -0.5, 0.375),
        "horizontal_exit_matrix": gaussian(splits[5], (HEAD_NUMBER * HEAD_WIDTH, FEATURE_SIZE), (HEAD_NUMBER * HEAD_WIDTH) ** -0.5, 0.375),
        "vertical_attend_matrix": gaussian(splits[6], (FEATURE_SIZE, 4 * HEAD_NUMBER * HEAD_WIDTH), FEATURE_SIZE ** -0.5, 0.375),
        "vertical_exit_matrix": gaussian(splits[7], (HEAD_NUMBER * HEAD_WIDTH, FEATURE_SIZE), (HEAD_NUMBER * HEAD_WIDTH) ** -0.5, 0.375),
        "averaged_product_flanks": gaussian(splits[8], (FEATURE_SIZE, 2 * FACTOR_FEATURES), FEATURE_SIZE ** -0.5, 0.375),
        "averaged_product_exit": gaussian(splits[9], (FACTOR_FEATURES * FACTOR_FEATURES, CZ), FACTOR_FEATURES ** -0.5, 1.0),
    }


def standardise_features(values):
    values = values.astype(jnp.float32)
    center = values - lax.optimization_barrier(jnp.mean(values, axis=-1, keepdims=True))
    spread = lax.optimization_barrier(jnp.mean(center * center, axis=-1, keepdims=True))
    return center * lax.rsqrt(spread + 1e-05)

def attend(normed, w_qkvg, w_out, bias):
    batch, length = (normed.shape[0], normed.shape[1])
    proj = jnp.einsum('blc,cf->blf', normed.astype(jnp.float32), w_qkvg.astype(jnp.float32))
    proj = proj.reshape(batch, length, 4, HEAD_NUMBER, HEAD_WIDTH)
    query = (proj[:, :, 0] * HEAD_WIDTH ** (-0.5)).astype(jnp.bfloat16)
    keys = proj[:, :, 1].astype(jnp.bfloat16)
    values = proj[:, :, 2].astype(jnp.bfloat16)
    gate = proj[:, :, 3]
    if bias is None:
        bias = jnp.zeros((HEAD_NUMBER, length, length), jnp.bfloat16)

    def one_head(items):
        qh, kh, vh, bh = items
        scores = jnp.einsum('bid,bjd->bij', qh.astype(jnp.float32), kh.astype(jnp.float32))
        scores = scores + bh.astype(jnp.float32)[None]
        weights = jax.nn.softmax(scores, axis=-1).astype(jnp.bfloat16)
        return jnp.einsum('bij,bjd->bid', weights.astype(jnp.float32), vh.astype(jnp.float32))
    heads = lax.map(one_head, (jnp.moveaxis(query, 2, 0), jnp.moveaxis(keys, 2, 0), jnp.moveaxis(values, 2, 0), bias))
    heads = jnp.moveaxis(heads, 0, 2)
    gated = (jax.nn.sigmoid(gate) * heads).astype(jnp.bfloat16).reshape(batch, length, HEAD_NUMBER * HEAD_WIDTH)
    return jnp.einsum('blk,kc->blc', gated.astype(jnp.float32), w_out.astype(jnp.float32))

def reference(homolog_tensor, couple_tensor, horizontal_drop_filter, couple_offset_matrix, horizontal_attend_matrix, horizontal_exit_matrix, vertical_attend_matrix, vertical_exit_matrix, averaged_product_flanks, averaged_product_exit):
    normed_pair = standardise_features(couple_tensor).astype(jnp.bfloat16)
    bias = jnp.einsum('ijz,zh->hij', normed_pair.astype(jnp.float32), couple_offset_matrix.astype(jnp.float32)).astype(jnp.bfloat16)
    starting_answer = standardise_features(homolog_tensor).astype(jnp.bfloat16)
    perform_refresh = attend(starting_answer, horizontal_attend_matrix, horizontal_exit_matrix, bias)
    homolog_later = (homolog_tensor.astype(jnp.float32) + horizontal_drop_filter.astype(jnp.float32) * (1.0 / 0.9) * perform_refresh).astype(jnp.bfloat16)
    column_layout = jnp.swapaxes(homolog_later, 0, 1)
    perform_refresh = attend(standardise_features(column_layout).astype(jnp.bfloat16), vertical_attend_matrix, vertical_exit_matrix, None)
    alignment_output = jnp.swapaxes((column_layout.astype(jnp.float32) + perform_refresh).astype(jnp.bfloat16), 0, 1)
    final_result = standardise_features(alignment_output).astype(jnp.bfloat16)
    factors = jnp.einsum('sic,cf->sif', final_result.astype(jnp.float32), averaged_product_flanks.astype(jnp.float32))
    left = factors[..., :FACTOR_FEATURES].astype(jnp.bfloat16)
    right = factors[..., FACTOR_FEATURES:].astype(jnp.bfloat16)

    def one_row(items):
        left_row, pair_row = items
        outer = jnp.einsum('sc,sjd->jcd', left_row.astype(jnp.float32), right.astype(jnp.float32)) / HOMOLOG_TOTAL
        outer = outer.astype(jnp.bfloat16).reshape(AMINO_TOTAL, FACTOR_FEATURES * FACTOR_FEATURES)
        change = jnp.dot(outer, averaged_product_exit, preferred_element_type=jnp.float32)
        return (pair_row.astype(jnp.float32) + change).astype(jnp.bfloat16)
    pair_output_state = lax.map(one_row, (jnp.swapaxes(left, 0, 1), couple_tensor))
    return (alignment_output, pair_output_state)
```

```python
import functools

import jax
import jax.numpy as jnp
from jax import lax
from jax.experimental import pallas as pl
from jax.experimental.pallas import tpu as pltpu
from jax.sharding import PartitionSpec as P

HEAD_NUMBER = 8
HEAD_WIDTH = 32
FACTOR_FEATURES = 32
LANES = 128
BF16 = jnp.bfloat16
F32 = jnp.float32


def standardise_features(values):
    values = values.astype(jnp.float32)
    center = values - jnp.mean(values, axis=-1, keepdims=True)
    spread = jnp.mean(center * center, axis=-1, keepdims=True)
    return center * lax.rsqrt(spread + 1e-05)


def attend(normed, w_qkvg, w_out, bias):
    batch, length = (normed.shape[0], normed.shape[1])
    proj = jnp.einsum("blc,cf->blf", normed, w_qkvg, preferred_element_type=jnp.float32)
    proj = proj.reshape(batch, length, 4, HEAD_NUMBER, HEAD_WIDTH)
    query = (proj[:, :, 0] * HEAD_WIDTH ** (-0.5)).astype(jnp.bfloat16)
    keys = proj[:, :, 1].astype(jnp.bfloat16)
    values = proj[:, :, 2].astype(jnp.bfloat16)
    gate = proj[:, :, 3]
    if bias is None:
        bias = jnp.zeros((HEAD_NUMBER, length, length), jnp.bfloat16)

    def one_head(items):
        qh, kh, vh, bh = items
        scores = jnp.einsum("bid,bjd->bij", qh, kh, preferred_element_type=jnp.float32)
        scores = scores + bh.astype(jnp.float32)[None]
        weights = jax.nn.softmax(scores, axis=-1).astype(jnp.bfloat16)
        return jnp.einsum("bij,bjd->bid", weights, vh, preferred_element_type=jnp.float32)

    heads = lax.map(
        one_head,
        (jnp.moveaxis(query, 2, 0), jnp.moveaxis(keys, 2, 0), jnp.moveaxis(values, 2, 0), bias),
    )
    heads = jnp.moveaxis(heads, 0, 2)
    gated = (
        (jax.nn.sigmoid(gate) * heads)
        .astype(jnp.bfloat16)
        .reshape(batch, length, HEAD_NUMBER * HEAD_WIDTH)
    )
    return jnp.einsum("blk,kc->blc", gated, w_out, preferred_element_type=jnp.float32)


def general_shards(
    homolog_tensor,
    couple_tensor,
    horizontal_drop_filter,
    couple_offset_matrix,
    horizontal_attend_matrix,
    horizontal_exit_matrix,
    vertical_attend_matrix,
    vertical_exit_matrix,
    averaged_product_flanks,
    averaged_product_exit,
):
    normed_pair = standardise_features(couple_tensor).astype(jnp.bfloat16)
    own_bias = jnp.einsum(
        "ijz,zh->hij", normed_pair, couple_offset_matrix, preferred_element_type=jnp.float32
    ).astype(jnp.bfloat16)
    bias = lax.all_gather(own_bias, "dap", axis=1, tiled=True)
    starting_answer = standardise_features(homolog_tensor).astype(jnp.bfloat16)
    perform_refresh = attend(
        starting_answer, horizontal_attend_matrix, horizontal_exit_matrix, bias
    )
    homolog_later = (
        homolog_tensor.astype(jnp.float32)
        + horizontal_drop_filter.astype(jnp.float32) * (1.0 / 0.9) * perform_refresh
    ).astype(jnp.bfloat16)
    incoming_blocks = lax.all_to_all(homolog_later, "dap", split_axis=1, concat_axis=0, tiled=True)
    column_layout = jnp.swapaxes(incoming_blocks, 0, 1)
    perform_refresh = attend(
        standardise_features(column_layout).astype(jnp.bfloat16),
        vertical_attend_matrix,
        vertical_exit_matrix,
        None,
    )
    alignment_output = jnp.swapaxes(
        (column_layout.astype(jnp.float32) + perform_refresh).astype(jnp.bfloat16), 0, 1
    )
    final_result = standardise_features(alignment_output).astype(jnp.bfloat16)
    factors = jnp.einsum(
        "sic,cf->sif", final_result, averaged_product_flanks, preferred_element_type=jnp.float32
    )
    left = factors[..., :FACTOR_FEATURES].astype(jnp.bfloat16)
    right = factors[..., FACTOR_FEATURES:].astype(jnp.bfloat16)
    total = left.shape[0]
    own_rows = left.shape[1]
    whole = lax.all_gather(right, "dap", axis=1, tiled=True)
    outer = jnp.einsum("sic,sjd->ijcd", left, whole, preferred_element_type=jnp.float32) / total
    outer = outer.astype(jnp.bfloat16).reshape(
        own_rows, whole.shape[1], FACTOR_FEATURES * FACTOR_FEATURES
    )
    change = jnp.einsum(
        "ijk,kz->ijz", outer, averaged_product_exit, preferred_element_type=jnp.float32
    )
    pair_output_state = (couple_tensor.astype(jnp.float32) + change).astype(jnp.bfloat16)
    return (alignment_output, pair_output_state)


def dot(a, b, ca=1, cb=0):
    return lax.dot_general(a, b, (((ca,), (cb,)), ((), ())), preferred_element_type=F32)


def iota(shape, axis):
    return lax.broadcasted_iota(jnp.int32, shape, axis)


def slot_device(me, slot, rounds):
    out = jnp.zeros_like(slot) + me
    for bit, mask in enumerate(rounds):
        out = out ^ (((slot >> bit) & 1) * mask)
    return out


def residue_order(me, length, own):
    half = length // 2
    place = iota((length, length), 0)
    other = (place >= half).astype(jnp.int32)
    rest = place - other * half
    parity = other ^ (me & 1)
    residue = ((rest // own) * 2 + parity) * own + rest % own
    return (iota((length, length), 1) == residue).astype(F32).astype(BF16)


def softmax_attention(q, k, v, bias_t, rows, groups):
    features = q.shape[1]
    per = LANES // HEAD_WIDTH
    head_of_lane = iota((rows, LANES), 1) // HEAD_WIDTH
    masks = [head_of_lane == t for t in range(per)]
    zero = jnp.zeros((rows, LANES), BF16)
    out = []
    for g in range(groups):
        parts = []
        for part in range(features // LANES):
            lanes = slice(part * LANES, (part + 1) * LANES)
            qh = q[g * rows : (g + 1) * rows, lanes]
            kh = k[g * rows : (g + 1) * rows, lanes]
            vh = v[g * rows : (g + 1) * rows, lanes]
            spread = jnp.concatenate([jnp.where(m, qh, zero) for m in masks], axis=0)
            scores = dot(kh, spread, 1, 1)
            if bias_t is not None:
                scores = scores + bias_t[:, part * per * rows : (part + 1) * per * rows]
            top = jnp.max(scores, axis=0, keepdims=True)
            e = jnp.exp(scores - top)
            w = (e / jnp.sum(e, axis=0, keepdims=True)).astype(BF16)
            o = dot(w, vh, 0, 0)
            acc = o[:rows]
            for t in range(1, per):
                acc = jnp.where(masks[t], o[t * rows : (t + 1) * rows], acc)
            parts.append(acc)
        out.append(jnp.concatenate(parts, axis=1))
    return jnp.concatenate(out, axis=0)


def gated_attention(x, w_ref, wo_ref, bias_t, rows, groups):
    features = x.shape[1]
    normed = standardise_features(x).astype(BF16)
    q = (dot(normed, w_ref[:, :features]) * HEAD_WIDTH ** (-0.5)).astype(BF16)
    k = dot(normed, w_ref[:, features : 2 * features]).astype(BF16)
    v = dot(normed, w_ref[:, 2 * features : 3 * features]).astype(BF16)
    o = softmax_attention(q, k, v, bias_t, rows, groups)
    gate = dot(normed, w_ref[:, 3 * features :])
    gated = (jax.nn.sigmoid(gate) * o).astype(BF16)
    return dot(gated, wo_ref[...])


def start_kernel(own, me_ref, msa_ref, pair_ref, wb_ref, out_ref):
    me = me_ref[0]
    seqs, length, features = msa_ref.shape
    order = residue_order(me, length, own)
    for s in range(seqs):
        out_ref[s * length : (s + 1) * length, :] = dot(order, msa_ref[s]).astype(BF16)
    zn = standardise_features(pair_ref[...]).astype(BF16)
    bias = dot(wb_ref[...], zn, 0, 1)
    pad = features - bias.shape[1]
    block = jnp.concatenate([bias, jnp.zeros((bias.shape[0], pad), F32)], axis=1)
    tail = out_ref.shape[0] - seqs * length - bias.shape[0]
    block = jnp.concatenate([block, jnp.zeros((tail, features), F32)], axis=0)
    out_ref[seqs * length :, :] = block.astype(BF16)


def row_kernel(
    rounds, seqs, own, me_ref, buf_ref, other_ref, w_ref, wo_ref, drop_ref, mine_ref, send_ref, acc_ref
):
    me = me_ref[0]
    slots = buf_ref.shape[0]
    length, features = drop_ref.shape
    half = length // 2
    order = residue_order(me, length, own)
    blocks = [buf_ref[k, seqs * length : seqs * length + HEAD_NUMBER, :LANES] for k in range(slots)]
    blocks += [other_ref[k] for k in range(slots)]
    blocks = jnp.concatenate([b.astype(F32) for b in blocks], axis=0).astype(BF16)
    shape = (2 * slots * HEAD_NUMBER, HEAD_NUMBER * length)
    row = iota(shape, 0)
    lane = iota(shape, 1)
    slot = row // HEAD_NUMBER
    cross = slot // slots
    chip = slot_device(me, slot % slots, rounds) >> 1
    base = (row % HEAD_NUMBER) * length + cross * half + chip * own
    bias_t = None
    for i in range(own):
        place = (lane == base + i).astype(F32).astype(BF16)
        part = dot(blocks, place, 0, 0)[i * length : (i + 1) * length]
        bias_t = part if bias_t is None else bias_t + part
    bias_t = dot(order, bias_t.astype(BF16))
    drop = dot(order, drop_ref[...].astype(F32).astype(BF16)) * (1.0 / 0.9)

    def body(t, carry):
        both = [buf_ref[2 * t + u, : seqs * length, :] for u in range(2)]
        x = jnp.concatenate(both, axis=0).astype(F32)
        refresh = gated_attention(x, w_ref, wo_ref, bias_t, length, 2 * seqs)
        tiled = jnp.concatenate([drop] * (2 * seqs), axis=0)
        later = (x + tiled * refresh).astype(BF16)
        size = 2 * seqs * length
        later = later.astype(F32)
        for part in range(features // LANES):
            lanes = slice(part * LANES, (part + 1) * LANES)
            acc_ref[part, pl.ds(pl.multiple_of(t * size, size), size), :] = later[:, lanes]
        return carry

    lax.fori_loop(0, slots // 2, body, 0)
    count = slots * seqs
    for r in range(length):
        for part in range(features // LANES):
            lanes = slice(part * LANES, (part + 1) * LANES)
            rows = acc_ref[part, pl.ds(r, count, stride=length), :].astype(BF16)
            if r < half:
                mine_ref[r, :, lanes] = rows
            else:
                send_ref[r - half, :, lanes] = rows


def column_kernel(
    rounds,
    seqs,
    own,
    me_ref,
    mine_ref,
    recv_ref,
    w_ref,
    wo_ref,
    flanks_ref,
    align_ref,
    left_ref,
    right_ref,
    al_ref,
    fac_ref,
):
    me = me_ref[0]
    half, count, features = mine_ref.shape
    total = 2 * count
    group = 4

    def body(t, carry):
        pieces = []
        for u in range(group):
            pieces += [mine_ref[group * t + u], recv_ref[group * t + u]]
        x = jnp.concatenate(pieces, axis=0).astype(F32)
        refresh = gated_attention(x, w_ref, wo_ref, None, total, group)
        aligned = (x + refresh).astype(BF16)
        normed = standardise_features(aligned).astype(BF16)
        factors = dot(normed, flanks_ref[...]).astype(BF16)
        for u in range(group):
            al_ref[group * t + u] = aligned[u * total : (u + 1) * total]
            fac_ref[group * t + u] = factors[u * total : (u + 1) * total]
            right_ref[group * t + u] = factors[u * total : (u + 1) * total, FACTOR_FEATURES:]
        return carry

    lax.fori_loop(0, half // group, body, 0)
    place = iota((total, total), 1)
    cross = place // count
    within = place % count
    device = slot_device(me, within // seqs, rounds) ^ cross
    order = (iota((total, total), 0) == device * seqs + within % seqs).astype(F32).astype(BF16)
    first = (me >> 1) * own
    for i in range(own):
        align_ref[i] = dot(order, al_ref[first + i]).astype(BF16)
        left_ref[i] = fac_ref[first + i][:, :FACTOR_FEATURES]


def small_shards(
    devices,
    homolog_tensor,
    couple_tensor,
    horizontal_drop_filter,
    couple_offset_matrix,
    horizontal_attend_matrix,
    horizontal_exit_matrix,
    vertical_attend_matrix,
    vertical_exit_matrix,
    averaged_product_flanks,
    averaged_product_exit,
):
    seqs, length, features = homolog_tensor.shape
    own = couple_tensor.shape[0]
    channels = couple_tensor.shape[2]
    half = length // 2
    slots = devices // 2
    count = slots * seqs
    total = 2 * count
    me = lax.axis_index("dap").astype(jnp.int32)
    me_arr = me.reshape(1)
    smem = pl.BlockSpec(memory_space=pltpu.SMEM)
    vmem = pl.BlockSpec(memory_space=pltpu.VMEM)
    rounds = []
    mask = devices // 2
    while mask > 1:
        rounds.append(mask)
        mask //= 2

    def swap(x, by):
        return lax.ppermute(x, "dap", [(i, i ^ by) for i in range(devices)])

    height = seqs * length + 16
    buf = pl.pallas_call(
        functools.partial(start_kernel, own),
        out_shape=jax.ShapeDtypeStruct((height, features), BF16),
        in_specs=[smem, vmem, vmem, vmem],
        out_specs=vmem,
    )(me_arr, homolog_tensor, couple_tensor.reshape(own * length, channels), couple_offset_matrix)
    buf = buf[None]
    for by in rounds:
        buf = jnp.concatenate([buf, swap(buf, by)], axis=0)
    other = swap(buf[:, seqs * length : seqs * length + HEAD_NUMBER, :LANES], 1)
    mine, send = pl.pallas_call(
        functools.partial(row_kernel, tuple(rounds), seqs, own),
        out_shape=[jax.ShapeDtypeStruct((half, count, features), BF16)] * 2,
        in_specs=[smem] + [vmem] * 5,
        out_specs=[vmem, vmem],
        scratch_shapes=[pltpu.VMEM((features // LANES, count * length, LANES), F32)],
    )(me_arr, buf, other, horizontal_attend_matrix, horizontal_exit_matrix, horizontal_drop_filter)
    recv = swap(send, 1)
    align, left, right = pl.pallas_call(
        functools.partial(column_kernel, tuple(rounds), seqs, own),
        out_shape=[
            jax.ShapeDtypeStruct((own, total, features), BF16),
            jax.ShapeDtypeStruct((own, total, FACTOR_FEATURES), BF16),
            jax.ShapeDtypeStruct((half, total, FACTOR_FEATURES), BF16),
        ],
        in_specs=[smem] + [vmem] * 5,
        out_specs=[vmem] * 3,
        scratch_shapes=[
            pltpu.VMEM((half, total, features), BF16),
            pltpu.VMEM((half, total, 2 * FACTOR_FEATURES), BF16),
        ],
    )(me_arr, mine, recv, vertical_attend_matrix, vertical_exit_matrix, averaged_product_flanks)
    alignment_output = jnp.swapaxes(align, 0, 1)
    right_other = swap(right, 1)
    right_other = jnp.concatenate([right_other[:, count:], right_other[:, :count]], axis=1)

    def change_of(factor):
        outer = jnp.einsum("isc,jsd->ijcd", left, factor, preferred_element_type=F32) / total
        outer = outer.astype(BF16).reshape(own, half, FACTOR_FEATURES * FACTOR_FEATURES)
        return jnp.einsum("ijk,kz->ijz", outer, averaged_product_exit, preferred_element_type=F32)

    mine_change = change_of(right)
    other_change = change_of(right_other)
    odd = (me & 1) == 1
    even_part = jnp.where(odd, other_change, mine_change).reshape(own, slots, 1, own, channels)
    odd_part = jnp.where(odd, mine_change, other_change).reshape(own, slots, 1, own, channels)
    change = jnp.concatenate([even_part, odd_part], axis=2).reshape(own, length, channels)
    pair_output_state = (couple_tensor.astype(F32) + change).astype(BF16)
    return (alignment_output, pair_output_state)


def solution(mesh):
    devices = mesh.shape["dap"]

    def shards(homolog_tensor, couple_tensor, *rest):
        seqs, length, features = homolog_tensor.shape
        own = couple_tensor.shape[0]
        power = devices >= 8 and devices & (devices - 1) == 0
        fits = devices * seqs <= 64 and length <= 32 and features % LANES == 0
        exact = own * devices == length and (own * length) <= LANES and (length // 2) % 4 == 0
        aligned = length % 16 == 0 and (devices // 2 * seqs) % 16 == 0
        if power and fits and exact and aligned:
            return small_shards(devices, homolog_tensor, couple_tensor, *rest)
        return general_shards(homolog_tensor, couple_tensor, *rest)

    placed = (
        P(("groups", "dap"), None, None),
        P(("groups", "dap"), None, None),
        P("groups", None),
        P(),
        P(),
        P(),
        P(),
        P(),
        P(),
        P(),
    )
    return jax.shard_map(
        shards,
        mesh=mesh,
        in_specs=placed,
        out_specs=(P("groups", "dap", None), P(("groups", "dap"), None, None)),
        check_vma=False,
    )
```

```python
import functools

import jax
import jax.numpy as jnp
from jax import lax
from jax.experimental import pallas as pl
from jax.experimental.pallas import tpu as pltpu
from jax.sharding import PartitionSpec as P

HEAD_NUMBER = 8
HEAD_WIDTH = 32
FACTOR_FEATURES = 32
LANES = 128
BF16 = jnp.bfloat16
F32 = jnp.float32


def standardise_features(values):
    values = values.astype(jnp.float32)
    center = values - jnp.mean(values, axis=-1, keepdims=True)
    spread = jnp.mean(center * center, axis=-1, keepdims=True)
    return center * lax.rsqrt(spread + 1e-05)


def attend(normed, w_qkvg, w_out, bias):
    batch, length = (normed.shape[0], normed.shape[1])
    proj = jnp.einsum("blc,cf->blf", normed, w_qkvg, preferred_element_type=jnp.float32)
    proj = proj.reshape(batch, length, 4, HEAD_NUMBER, HEAD_WIDTH)
    query = (proj[:, :, 0] * HEAD_WIDTH ** (-0.5)).astype(jnp.bfloat16)
    keys = proj[:, :, 1].astype(jnp.bfloat16)
    values = proj[:, :, 2].astype(jnp.bfloat16)
    gate = proj[:, :, 3]
    if bias is None:
        bias = jnp.zeros((HEAD_NUMBER, length, length), jnp.bfloat16)

    def one_head(items):
        qh, kh, vh, bh = items
        scores = jnp.einsum("bid,bjd->bij", qh, kh, preferred_element_type=jnp.float32)
        scores = scores + bh.astype(jnp.float32)[None]
        weights = jax.nn.softmax(scores, axis=-1).astype(jnp.bfloat16)
        return jnp.einsum("bij,bjd->bid", weights, vh, preferred_element_type=jnp.float32)

    heads = lax.map(
        one_head,
        (jnp.moveaxis(query, 2, 0), jnp.moveaxis(keys, 2, 0), jnp.moveaxis(values, 2, 0), bias),
    )
    heads = jnp.moveaxis(heads, 0, 2)
    gated = (
        (jax.nn.sigmoid(gate) * heads)
        .astype(jnp.bfloat16)
        .reshape(batch, length, HEAD_NUMBER * HEAD_WIDTH)
    )
    return jnp.einsum("blk,kc->blc", gated, w_out, preferred_element_type=jnp.float32)


def general_shards(
    homolog_tensor,
    couple_tensor,
    horizontal_drop_filter,
    couple_offset_matrix,
    horizontal_attend_matrix,
    horizontal_exit_matrix,
    vertical_attend_matrix,
    vertical_exit_matrix,
    averaged_product_flanks,
    averaged_product_exit,
):
    normed_pair = standardise_features(couple_tensor).astype(jnp.bfloat16)
    own_bias = jnp.einsum(
        "ijz,zh->hij", normed_pair, couple_offset_matrix, preferred_element_type=jnp.float32
    ).astype(jnp.bfloat16)
    bias = lax.all_gather(own_bias, "dap", axis=1, tiled=True)
    starting_answer = standardise_features(homolog_tensor).astype(jnp.bfloat16)
    perform_refresh = attend(
        starting_answer, horizontal_attend_matrix, horizontal_exit_matrix, bias
    )
    homolog_later = (
        homolog_tensor.astype(jnp.float32)
        + horizontal_drop_filter.astype(jnp.float32) * (1.0 / 0.9) * perform_refresh
    ).astype(jnp.bfloat16)
    incoming_blocks = lax.all_to_all(homolog_later, "dap", split_axis=1, concat_axis=0, tiled=True)
    column_layout = jnp.swapaxes(incoming_blocks, 0, 1)
    perform_refresh = attend(
        standardise_features(column_layout).astype(jnp.bfloat16),
        vertical_attend_matrix,
        vertical_exit_matrix,
        None,
    )
    alignment_output = jnp.swapaxes(
        (column_layout.astype(jnp.float32) + perform_refresh).astype(jnp.bfloat16), 0, 1
    )
    final_result = standardise_features(alignment_output).astype(jnp.bfloat16)
    factors = jnp.einsum(
        "sic,cf->sif", final_result, averaged_product_flanks, preferred_element_type=jnp.float32
    )
    left = factors[..., :FACTOR_FEATURES].astype(jnp.bfloat16)
    right = factors[..., FACTOR_FEATURES:].astype(jnp.bfloat16)
    total = left.shape[0]
    own_rows = left.shape[1]
    whole = lax.all_gather(right, "dap", axis=1, tiled=True)
    outer = jnp.einsum("sic,sjd->ijcd", left, whole, preferred_element_type=jnp.float32) / total
    outer = outer.astype(jnp.bfloat16).reshape(
        own_rows, whole.shape[1], FACTOR_FEATURES * FACTOR_FEATURES
    )
    change = jnp.einsum(
        "ijk,kz->ijz", outer, averaged_product_exit, preferred_element_type=jnp.float32
    )
    pair_output_state = (couple_tensor.astype(jnp.float32) + change).astype(jnp.bfloat16)
    return (alignment_output, pair_output_state)


def dot(a, b, ca=1, cb=0):
    return lax.dot_general(a, b, (((ca,), (cb,)), ((), ())), preferred_element_type=F32)


def iota(shape, axis):
    return lax.broadcasted_iota(jnp.int32, shape, axis)


def slot_device(me, slot, rounds):
    out = jnp.zeros_like(slot) + me
    for bit, mask in enumerate(rounds):
        out = out ^ (((slot >> bit) & 1) * mask)
    return out


def residue_order(me, length, own):
    half = length // 2
    place = iota((length, length), 0)
    other = (place >= half).astype(jnp.int32)
    rest = place - other * half
    parity = other ^ (me & 1)
    residue = ((rest // own) * 2 + parity) * own + rest % own
    return (iota((length, length), 1) == residue).astype(F32).astype(BF16)


def softmax_attention(q, k, v, bias_t, rows, groups):
    features = q.shape[1]
    per = LANES // HEAD_WIDTH
    head_of_lane = iota((rows, LANES), 1) // HEAD_WIDTH
    masks = [head_of_lane == t for t in range(per)]
    zero = jnp.zeros((rows, LANES), BF16)
    units = [(g, part) for g in range(groups) for part in range(features // LANES)]

    def piece(x, unit):
        g, part = unit
        return x[g * rows : (g + 1) * rows, part * LANES : (part + 1) * LANES]

    scores = []
    for unit in units:
        qh = piece(q, unit)
        spread = jnp.concatenate([jnp.where(m, qh, zero) for m in masks], axis=0)
        scores.append(dot(piece(k, unit), spread, 1, 1))
    scores = jnp.concatenate(scores, axis=1)
    if bias_t is not None:
        scores = scores + jnp.concatenate([bias_t] * groups, axis=1)
    e = jnp.exp(scores - jnp.max(scores, axis=0, keepdims=True))
    w = (e * (1.0 / jnp.sum(e, axis=0, keepdims=True))).astype(BF16)
    width = per * rows
    parts = []
    for n, unit in enumerate(units):
        o = dot(w[:, n * width : (n + 1) * width], piece(v, unit), 0, 0)
        acc = o[:rows]
        for t in range(1, per):
            acc = jnp.where(masks[t], o[t * rows : (t + 1) * rows], acc)
        parts.append(acc)
    count = features // LANES
    return jnp.concatenate(
        [jnp.concatenate(parts[g * count : (g + 1) * count], axis=1) for g in range(groups)], axis=0
    )


def gated_attention(x, w_ref, wo_ref, bias_t, rows, groups):
    features = x.shape[1]
    normed = standardise_features(x).astype(BF16)
    q = (dot(normed, w_ref[:, :features]) * HEAD_WIDTH ** (-0.5)).astype(BF16)
    k = dot(normed, w_ref[:, features : 2 * features]).astype(BF16)
    v = dot(normed, w_ref[:, 2 * features : 3 * features]).astype(BF16)
    o = softmax_attention(q, k, v, bias_t, rows, groups)
    gate = dot(normed, w_ref[:, 3 * features :])
    gated = (jax.nn.sigmoid(gate) * o).astype(BF16)
    return dot(gated, wo_ref[...])


def start_kernel(own, me_ref, msa_ref, pair_ref, wb_ref, out_ref):
    me = me_ref[0]
    seqs, length, features = msa_ref.shape
    order = residue_order(me, length, own)
    for s in range(seqs):
        out_ref[s * length : (s + 1) * length, :] = dot(order, msa_ref[s]).astype(BF16)
    zn = standardise_features(pair_ref[...]).astype(BF16)
    bias = dot(wb_ref[...], zn, 0, 1)
    pad = features - bias.shape[1]
    block = jnp.concatenate([bias, jnp.zeros((bias.shape[0], pad), F32)], axis=1)
    tail = out_ref.shape[0] - seqs * length - bias.shape[0]
    block = jnp.concatenate([block, jnp.zeros((tail, features), F32)], axis=0)
    out_ref[seqs * length :, :] = block.astype(BF16)


def row_kernel(
    rounds, seqs, own, me_ref, buf_ref, other_ref, w_ref, wo_ref, drop_ref, mine_ref, send_ref, acc_ref
):
    me = me_ref[0]
    slots = buf_ref.shape[0]
    length, features = drop_ref.shape
    half = length // 2
    order = residue_order(me, length, own)
    blocks = [buf_ref[k, seqs * length : seqs * length + HEAD_NUMBER, :LANES] for k in range(slots)]
    blocks += [other_ref[k] for k in range(slots)]
    blocks = jnp.concatenate([b.astype(F32) for b in blocks], axis=0).astype(BF16)
    shape = (2 * slots * HEAD_NUMBER, HEAD_NUMBER * length)
    row = iota(shape, 0)
    lane = iota(shape, 1)
    slot = row // HEAD_NUMBER
    cross = slot // slots
    chip = slot_device(me, slot % slots, rounds) >> 1
    base = (row % HEAD_NUMBER) * length + cross * half + chip * own
    bias_t = None
    for i in range(own):
        place = (lane == base + i).astype(F32).astype(BF16)
        part = dot(blocks, place, 0, 0)[i * length : (i + 1) * length]
        bias_t = part if bias_t is None else bias_t + part
    bias_t = dot(order, bias_t.astype(BF16))
    drop = dot(order, drop_ref[...].astype(F32).astype(BF16)) * (1.0 / 0.9)

    batch = 2 * seqs
    size = batch * length
    row = iota((size, size), 0)
    turn = (iota((size, size), 1) == (row % batch) * length + row // batch).astype(F32).astype(BF16)

    def body(t, carry):
        both = [buf_ref[2 * t + u, : seqs * length, :] for u in range(2)]
        x = jnp.concatenate(both, axis=0).astype(F32)
        refresh = gated_attention(x, w_ref, wo_ref, bias_t, length, batch)
        tiled = jnp.concatenate([drop] * batch, axis=0)
        later = (x + tiled * refresh).astype(BF16)
        turned = dot(turn, later).reshape(length, batch, features)
        acc_ref[:, pl.ds(pl.multiple_of(t * batch, batch), batch), :] = turned
        return carry

    lax.fori_loop(0, slots // 2, body, 0)
    mine_ref[...] = acc_ref[:half].astype(BF16)
    send_ref[...] = acc_ref[half:].astype(BF16)


def column_kernel(
    rounds,
    seqs,
    own,
    me_ref,
    mine_ref,
    recv_ref,
    w_ref,
    wo_ref,
    flanks_ref,
    align_ref,
    left_ref,
    right_ref,
    al_ref,
    fac_ref,
):
    me = me_ref[0]
    half, count, features = mine_ref.shape
    total = 2 * count
    group = 4

    def body(t, carry):
        pieces = []
        for u in range(group):
            pieces += [mine_ref[group * t + u], recv_ref[group * t + u]]
        x = jnp.concatenate(pieces, axis=0).astype(F32)
        refresh = gated_attention(x, w_ref, wo_ref, None, total, group)
        aligned = (x + refresh).astype(BF16)
        normed = standardise_features(aligned).astype(BF16)
        factors = dot(normed, flanks_ref[...]).astype(BF16)
        for u in range(group):
            al_ref[group * t + u] = aligned[u * total : (u + 1) * total]
            fac_ref[group * t + u] = factors[u * total : (u + 1) * total]
            right_ref[group * t + u] = factors[u * total : (u + 1) * total, FACTOR_FEATURES:]
        return carry

    lax.fori_loop(0, half // group, body, 0)
    place = iota((total, total), 1)
    cross = place // count
    within = place % count
    device = slot_device(me, within // seqs, rounds) ^ cross
    order = (iota((total, total), 0) == device * seqs + within % seqs).astype(F32).astype(BF16)
    first = (me >> 1) * own
    for i in range(own):
        align_ref[i] = dot(order, al_ref[first + i]).astype(BF16)
        left_ref[i] = fac_ref[first + i][:, :FACTOR_FEATURES]


def small_shards(
    devices,
    homolog_tensor,
    couple_tensor,
    horizontal_drop_filter,
    couple_offset_matrix,
    horizontal_attend_matrix,
    horizontal_exit_matrix,
    vertical_attend_matrix,
    vertical_exit_matrix,
    averaged_product_flanks,
    averaged_product_exit,
):
    seqs, length, features = homolog_tensor.shape
    own = couple_tensor.shape[0]
    channels = couple_tensor.shape[2]
    half = length // 2
    slots = devices // 2
    count = slots * seqs
    total = 2 * count
    me = lax.axis_index("dap").astype(jnp.int32)
    me_arr = me.reshape(1)
    smem = pl.BlockSpec(memory_space=pltpu.SMEM)
    vmem = pl.BlockSpec(memory_space=pltpu.VMEM)
    params = pltpu.CompilerParams(vmem_limit_bytes=24 * 1024 * 1024)
    rounds = []
    mask = devices // 2
    while mask > 1:
        rounds.append(mask)
        mask //= 2

    def swap(x, by):
        return lax.ppermute(x, "dap", [(i, i ^ by) for i in range(devices)])

    height = seqs * length + 16
    buf = pl.pallas_call(
        functools.partial(start_kernel, own),
        out_shape=jax.ShapeDtypeStruct((height, features), BF16),
        in_specs=[smem, vmem, vmem, vmem],
        out_specs=vmem,
        compiler_params=params,
    )(me_arr, homolog_tensor, couple_tensor.reshape(own * length, channels), couple_offset_matrix)
    buf = buf[None]
    for by in rounds:
        buf = jnp.concatenate([buf, swap(buf, by)], axis=0)
    other = swap(buf[:, seqs * length : seqs * length + HEAD_NUMBER, :LANES], 1)
    mine, send = pl.pallas_call(
        functools.partial(row_kernel, tuple(rounds), seqs, own),
        out_shape=[jax.ShapeDtypeStruct((half, count, features), BF16)] * 2,
        in_specs=[smem] + [vmem] * 5,
        out_specs=[vmem, vmem],
        scratch_shapes=[pltpu.VMEM((length, count, features), F32)],
        compiler_params=params,
    )(me_arr, buf, other, horizontal_attend_matrix, horizontal_exit_matrix, horizontal_drop_filter)
    recv = swap(send, 1)
    align, left, right = pl.pallas_call(
        functools.partial(column_kernel, tuple(rounds), seqs, own),
        out_shape=[
            jax.ShapeDtypeStruct((own, total, features), BF16),
            jax.ShapeDtypeStruct((own, total, FACTOR_FEATURES), BF16),
            jax.ShapeDtypeStruct((half, total, FACTOR_FEATURES), BF16),
        ],
        in_specs=[smem] + [vmem] * 5,
        out_specs=[vmem] * 3,
        scratch_shapes=[
            pltpu.VMEM((half, total, features), BF16),
            pltpu.VMEM((half, total, 2 * FACTOR_FEATURES), BF16),
        ],
        compiler_params=params,
    )(me_arr, mine, recv, vertical_attend_matrix, vertical_exit_matrix, averaged_product_flanks)
    alignment_output = jnp.swapaxes(align, 0, 1)
    right_other = swap(right, 1)
    right_other = jnp.concatenate([right_other[:, count:], right_other[:, :count]], axis=1)

    def change_of(factor):
        outer = jnp.einsum("isc,jsd->ijcd", left, factor, preferred_element_type=F32) / total
        outer = outer.astype(BF16).reshape(own, half, FACTOR_FEATURES * FACTOR_FEATURES)
        return jnp.einsum("ijk,kz->ijz", outer, averaged_product_exit, preferred_element_type=F32)

    mine_change = change_of(right)
    other_change = change_of(right_other)
    odd = (me & 1) == 1
    even_part = jnp.where(odd, other_change, mine_change).reshape(own, slots, 1, own, channels)
    odd_part = jnp.where(odd, mine_change, other_change).reshape(own, slots, 1, own, channels)
    change = jnp.concatenate([even_part, odd_part], axis=2).reshape(own, length, channels)
    pair_output_state = (couple_tensor.astype(F32) + change).astype(BF16)
    return (alignment_output, pair_output_state)


def solution(mesh):
    devices = mesh.shape["dap"]

    def shards(homolog_tensor, couple_tensor, *rest):
        seqs, length, features = homolog_tensor.shape
        own = couple_tensor.shape[0]
        power = devices >= 8 and devices & (devices - 1) == 0
        fits = devices * seqs <= 64 and length <= 32 and features % LANES == 0
        exact = own * devices == length and (own * length) <= LANES and (length // 2) % 4 == 0
        aligned = length % 16 == 0 and (devices // 2 * seqs) % 16 == 0
        if power and fits and exact and aligned:
            return small_shards(devices, homolog_tensor, couple_tensor, *rest)
        return general_shards(homolog_tensor, couple_tensor, *rest)

    placed = (
        P(("groups", "dap"), None, None),
        P(("groups", "dap"), None, None),
        P("groups", None),
        P(),
        P(),
        P(),
        P(),
        P(),
        P(),
        P(),
    )
    return jax.shard_map(
        shards,
        mesh=mesh,
        in_specs=placed,
        out_specs=(P("groups", "dap", None), P(("groups", "dap"), None, None)),
        check_vma=False,
    )
```

```python
import functools

import jax
import jax.numpy as jnp
from jax import lax
from jax.experimental import pallas as pl
from jax.experimental.pallas import tpu as pltpu
from jax.sharding import PartitionSpec as P

HEAD_NUMBER = 8
HEAD_WIDTH = 32
FACTOR_FEATURES = 32
LANES = 128
BF16 = jnp.bfloat16
F32 = jnp.float32


def standardise_features(values):
    values = values.astype(jnp.float32)
    center = values - jnp.mean(values, axis=-1, keepdims=True)
    spread = jnp.mean(center * center, axis=-1, keepdims=True)
    return center * lax.rsqrt(spread + 1e-05)


def attend(normed, w_qkvg, w_out, bias):
    batch, length = (normed.shape[0], normed.shape[1])
    proj = jnp.einsum("blc,cf->blf", normed, w_qkvg, preferred_element_type=jnp.float32)
    proj = proj.reshape(batch, length, 4, HEAD_NUMBER, HEAD_WIDTH)
    query = (proj[:, :, 0] * HEAD_WIDTH ** (-0.5)).astype(jnp.bfloat16)
    keys = proj[:, :, 1].astype(jnp.bfloat16)
    values = proj[:, :, 2].astype(jnp.bfloat16)
    gate = proj[:, :, 3]
    if bias is None:
        bias = jnp.zeros((HEAD_NUMBER, length, length), jnp.bfloat16)

    def one_head(items):
        qh, kh, vh, bh = items
        scores = jnp.einsum("bid,bjd->bij", qh, kh, preferred_element_type=jnp.float32)
        scores = scores + bh.astype(jnp.float32)[None]
        weights = jax.nn.softmax(scores, axis=-1).astype(jnp.bfloat16)
        return jnp.einsum("bij,bjd->bid", weights, vh, preferred_element_type=jnp.float32)

    heads = lax.map(
        one_head,
        (jnp.moveaxis(query, 2, 0), jnp.moveaxis(keys, 2, 0), jnp.moveaxis(values, 2, 0), bias),
    )
    heads = jnp.moveaxis(heads, 0, 2)
    gated = (
        (jax.nn.sigmoid(gate) * heads)
        .astype(jnp.bfloat16)
        .reshape(batch, length, HEAD_NUMBER * HEAD_WIDTH)
    )
    return jnp.einsum("blk,kc->blc", gated, w_out, preferred_element_type=jnp.float32)


def general_shards(
    homolog_tensor,
    couple_tensor,
    horizontal_drop_filter,
    couple_offset_matrix,
    horizontal_attend_matrix,
    horizontal_exit_matrix,
    vertical_attend_matrix,
    vertical_exit_matrix,
    averaged_product_flanks,
    averaged_product_exit,
):
    normed_pair = standardise_features(couple_tensor).astype(jnp.bfloat16)
    own_bias = jnp.einsum(
        "ijz,zh->hij", normed_pair, couple_offset_matrix, preferred_element_type=jnp.float32
    ).astype(jnp.bfloat16)
    bias = lax.all_gather(own_bias, "dap", axis=1, tiled=True)
    starting_answer = standardise_features(homolog_tensor).astype(jnp.bfloat16)
    perform_refresh = attend(
        starting_answer, horizontal_attend_matrix, horizontal_exit_matrix, bias
    )
    homolog_later = (
        homolog_tensor.astype(jnp.float32)
        + horizontal_drop_filter.astype(jnp.float32) * (1.0 / 0.9) * perform_refresh
    ).astype(jnp.bfloat16)
    incoming_blocks = lax.all_to_all(homolog_later, "dap", split_axis=1, concat_axis=0, tiled=True)
    column_layout = jnp.swapaxes(incoming_blocks, 0, 1)
    perform_refresh = attend(
        standardise_features(column_layout).astype(jnp.bfloat16),
        vertical_attend_matrix,
        vertical_exit_matrix,
        None,
    )
    alignment_output = jnp.swapaxes(
        (column_layout.astype(jnp.float32) + perform_refresh).astype(jnp.bfloat16), 0, 1
    )
    final_result = standardise_features(alignment_output).astype(jnp.bfloat16)
    factors = jnp.einsum(
        "sic,cf->sif", final_result, averaged_product_flanks, preferred_element_type=jnp.float32
    )
    left = factors[..., :FACTOR_FEATURES].astype(jnp.bfloat16)
    right = factors[..., FACTOR_FEATURES:].astype(jnp.bfloat16)
    total = left.shape[0]
    own_rows = left.shape[1]
    whole = lax.all_gather(right, "dap", axis=1, tiled=True)
    outer = jnp.einsum("sic,sjd->ijcd", left, whole, preferred_element_type=jnp.float32) / total
    outer = outer.astype(jnp.bfloat16).reshape(
        own_rows, whole.shape[1], FACTOR_FEATURES * FACTOR_FEATURES
    )
    change = jnp.einsum(
        "ijk,kz->ijz", outer, averaged_product_exit, preferred_element_type=jnp.float32
    )
    pair_output_state = (couple_tensor.astype(jnp.float32) + change).astype(jnp.bfloat16)
    return (alignment_output, pair_output_state)


def dot(a, b, ca=1, cb=0):
    return lax.dot_general(a, b, (((ca,), (cb,)), ((), ())), preferred_element_type=F32)


def iota(shape, axis):
    return lax.broadcasted_iota(jnp.int32, shape, axis)


def slot_device(me, slot, rounds):
    out = jnp.zeros_like(slot) + me
    for bit, mask in enumerate(rounds):
        out = out ^ (((slot >> bit) & 1) * mask)
    return out


def residue_order(me, length, own):
    half = length // 2
    place = iota((length, length), 0)
    other = (place >= half).astype(jnp.int32)
    rest = place - other * half
    parity = other ^ (me & 1)
    residue = ((rest // own) * 2 + parity) * own + rest % own
    return (iota((length, length), 1) == residue).astype(F32).astype(BF16)


def softmax_attention(q, k, v, bias_t, rows, groups):
    features = q.shape[1]
    per = LANES // HEAD_WIDTH
    head_of_lane = iota((rows, LANES), 1) // HEAD_WIDTH
    masks = [head_of_lane == t for t in range(per)]
    zero = jnp.zeros((rows, LANES), BF16)
    units = [(g, part) for g in range(groups) for part in range(features // LANES)]

    def piece(x, unit):
        g, part = unit
        return x[g * rows : (g + 1) * rows, part * LANES : (part + 1) * LANES]

    scores = []
    for unit in units:
        qh = piece(q, unit)
        spread = jnp.concatenate([jnp.where(m, qh, zero) for m in masks], axis=0)
        scores.append(dot(piece(k, unit), spread, 1, 1))
    scores = jnp.concatenate(scores, axis=1)
    if bias_t is not None:
        scores = scores + jnp.concatenate([bias_t] * groups, axis=1)
    e = jnp.exp(scores - jnp.max(scores, axis=0, keepdims=True))
    w = (e * (1.0 / jnp.sum(e, axis=0, keepdims=True))).astype(BF16)
    width = per * rows
    parts = []
    for n, unit in enumerate(units):
        o = dot(w[:, n * width : (n + 1) * width], piece(v, unit), 0, 0)
        acc = o[:rows]
        for t in range(1, per):
            acc = jnp.where(masks[t], o[t * rows : (t + 1) * rows], acc)
        parts.append(acc)
    count = features // LANES
    return jnp.concatenate(
        [jnp.concatenate(parts[g * count : (g + 1) * count], axis=1) for g in range(groups)], axis=0
    )


def gated_attention(x, w_ref, wo_ref, bias_t, rows, groups):
    features = x.shape[1]
    normed = standardise_features(x).astype(BF16)
    q = (dot(normed, w_ref[:, :features]) * HEAD_WIDTH ** (-0.5)).astype(BF16)
    k = dot(normed, w_ref[:, features : 2 * features]).astype(BF16)
    v = dot(normed, w_ref[:, 2 * features : 3 * features]).astype(BF16)
    o = softmax_attention(q, k, v, bias_t, rows, groups)
    gate = dot(normed, w_ref[:, 3 * features :])
    gated = (jax.nn.sigmoid(gate) * o).astype(BF16)
    return dot(gated, wo_ref[...])


def start_kernel(own, me_ref, msa_hbm, pair_hbm, wb_hbm, out_ref, msa_ref, pair_ref, wb_ref, sems):
    copies = [
        pltpu.make_async_copy(pair_hbm, pair_ref, sems.at[0]),
        pltpu.make_async_copy(wb_hbm, wb_ref, sems.at[1]),
        pltpu.make_async_copy(msa_hbm, msa_ref, sems.at[2]),
    ]
    for copy in copies:
        copy.start()
    me = me_ref[0]
    seqs, length, features = msa_ref.shape
    order = residue_order(me, length, own)
    copies[0].wait()
    copies[1].wait()
    zn = standardise_features(pair_ref[...]).astype(BF16)
    bias = dot(wb_ref[...], zn, 1, 1)
    pad = features - bias.shape[1]
    block = jnp.concatenate([bias, jnp.zeros((bias.shape[0], pad), F32)], axis=1)
    tail = out_ref.shape[0] - seqs * length - bias.shape[0]
    block = jnp.concatenate([block, jnp.zeros((tail, features), F32)], axis=0)
    out_ref[seqs * length :, :] = block.astype(BF16)
    copies[2].wait()
    for s in range(seqs):
        out_ref[s * length : (s + 1) * length, :] = dot(order, msa_ref[s]).astype(BF16)


def row_kernel(
    rounds, seqs, own, me_ref, buf_ref, other_ref, w_ref, wo_ref, drop_ref, mine_ref, send_ref, acc_ref
):
    me = me_ref[0]
    slots = buf_ref.shape[0]
    length, features = drop_ref.shape
    half = length // 2
    order = residue_order(me, length, own)
    blocks = [buf_ref[k, seqs * length : seqs * length + HEAD_NUMBER, :LANES] for k in range(slots)]
    blocks += [other_ref[k] for k in range(slots)]
    blocks = jnp.concatenate([b.astype(F32) for b in blocks], axis=0).astype(BF16)
    shape = (2 * slots * HEAD_NUMBER, HEAD_NUMBER * length)
    row = iota(shape, 0)
    lane = iota(shape, 1)
    slot = row // HEAD_NUMBER
    cross = slot // slots
    chip = slot_device(me, slot % slots, rounds) >> 1
    base = (row % HEAD_NUMBER) * length + cross * half + chip * own
    bias_t = None
    for i in range(own):
        place = (lane == base + i).astype(F32).astype(BF16)
        part = dot(blocks, place, 0, 0)[i * length : (i + 1) * length]
        bias_t = part if bias_t is None else bias_t + part
    bias_t = dot(order, bias_t.astype(BF16))
    drop = dot(order, drop_ref[...].astype(F32).astype(BF16)) * (1.0 / 0.9)

    batch = 2 * seqs
    size = batch * length
    row = iota((size, size), 0)
    turn = (iota((size, size), 1) == (row % batch) * length + row // batch).astype(F32).astype(BF16)

    def body(t, carry):
        both = [buf_ref[2 * t + u, : seqs * length, :] for u in range(2)]
        x = jnp.concatenate(both, axis=0).astype(F32)
        refresh = gated_attention(x, w_ref, wo_ref, bias_t, length, batch)
        tiled = jnp.concatenate([drop] * batch, axis=0)
        later = (x + tiled * refresh).astype(BF16)
        turned = dot(turn, later).reshape(length, batch, features)
        acc_ref[:, pl.ds(pl.multiple_of(t * batch, batch), batch), :] = turned
        return carry

    lax.fori_loop(0, slots // 2, body, 0)
    mine_ref[...] = acc_ref[:half].astype(BF16)
    send_ref[...] = acc_ref[half:].astype(BF16)


def column_kernel(
    rounds,
    seqs,
    own,
    me_ref,
    mine_ref,
    recv_ref,
    w_ref,
    wo_ref,
    flanks_ref,
    align_ref,
    left_ref,
    right_ref,
    al_ref,
    fac_ref,
):
    me = me_ref[0]
    half, count, features = mine_ref.shape
    total = 2 * count
    group = 4

    def body(t, carry):
        pieces = []
        for u in range(group):
            pieces += [mine_ref[group * t + u], recv_ref[group * t + u]]
        x = jnp.concatenate(pieces, axis=0).astype(F32)
        refresh = gated_attention(x, w_ref, wo_ref, None, total, group)
        aligned = (x + refresh).astype(BF16)
        normed = standardise_features(aligned).astype(BF16)
        factors = dot(normed, flanks_ref[...], 1, 1).astype(BF16)
        for u in range(group):
            al_ref[group * t + u] = aligned[u * total : (u + 1) * total]
            fac_ref[group * t + u] = factors[u * total : (u + 1) * total]
            right_ref[group * t + u] = factors[u * total : (u + 1) * total, FACTOR_FEATURES:]
        return carry

    lax.fori_loop(0, half // group, body, 0)
    place = iota((total, total), 1)
    cross = place // count
    within = place % count
    device = slot_device(me, within // seqs, rounds) ^ cross
    order = (iota((total, total), 0) == device * seqs + within % seqs).astype(F32).astype(BF16)
    first = (me >> 1) * own
    for i in range(own):
        align_ref[i] = dot(order, al_ref[first + i]).astype(BF16)
        left_ref[i] = fac_ref[first + i][:, :FACTOR_FEATURES]


def small_shards(
    devices,
    homolog_tensor,
    couple_tensor,
    horizontal_drop_filter,
    couple_offset_matrix,
    horizontal_attend_matrix,
    horizontal_exit_matrix,
    vertical_attend_matrix,
    vertical_exit_matrix,
    averaged_product_flanks,
    averaged_product_exit,
):
    seqs, length, features = homolog_tensor.shape
    own = couple_tensor.shape[0]
    channels = couple_tensor.shape[2]
    half = length // 2
    slots = devices // 2
    count = slots * seqs
    total = 2 * count
    me = lax.axis_index("dap").astype(jnp.int32)
    me_arr = me.reshape(1)
    smem = pl.BlockSpec(memory_space=pltpu.SMEM)
    vmem = pl.BlockSpec(memory_space=pltpu.VMEM)
    params = pltpu.CompilerParams(vmem_limit_bytes=24 * 1024 * 1024)
    rounds = []
    mask = devices // 2
    while mask > 1:
        rounds.append(mask)
        mask //= 2

    def swap(x, by):
        return lax.ppermute(x, "dap", [(i, i ^ by) for i in range(devices)])

    height = seqs * length + 16
    hbm = pl.BlockSpec(memory_space=pltpu.HBM)
    new = pl.pallas_call(
        functools.partial(start_kernel, own),
        out_shape=jax.ShapeDtypeStruct((height, features), BF16),
        in_specs=[smem, hbm, hbm, hbm],
        out_specs=vmem,
        scratch_shapes=[
            pltpu.VMEM((seqs, length, features), BF16),
            pltpu.VMEM((own * length, channels), BF16),
            pltpu.VMEM((HEAD_NUMBER, channels), BF16),
            pltpu.SemaphoreType.DMA((3,)),
        ],
        compiler_params=params,
    )(me_arr, homolog_tensor, couple_tensor.reshape(own * length, channels), couple_offset_matrix.T)
    new = new[None]
    near = [new]
    far = []
    for by in rounds[:-1]:
        got = swap(jnp.concatenate(near, axis=0), by)
        far.append(swap(new, rounds[-1]))
        near.append(got)
        new = got
    far.append(swap(new, rounds[-1]))
    buf = jnp.concatenate(near + far, axis=0)
    other = swap(buf[:, seqs * length : seqs * length + HEAD_NUMBER, :LANES], 1)
    mine, send = pl.pallas_call(
        functools.partial(row_kernel, tuple(rounds), seqs, own),
        out_shape=[jax.ShapeDtypeStruct((half, count, features), BF16)] * 2,
        in_specs=[smem] + [vmem] * 5,
        out_specs=[vmem, vmem],
        scratch_shapes=[pltpu.VMEM((length, count, features), F32)],
        compiler_params=params,
    )(me_arr, buf, other, horizontal_attend_matrix, horizontal_exit_matrix, horizontal_drop_filter)
    recv = swap(send, 1)
    align, left, right = pl.pallas_call(
        functools.partial(column_kernel, tuple(rounds), seqs, own),
        out_shape=[
            jax.ShapeDtypeStruct((own, total, features), BF16),
            jax.ShapeDtypeStruct((own, total, FACTOR_FEATURES), BF16),
            jax.ShapeDtypeStruct((half, total, FACTOR_FEATURES), BF16),
        ],
        in_specs=[smem] + [vmem] * 5,
        out_specs=[vmem] * 3,
        scratch_shapes=[
            pltpu.VMEM((half, total, features), BF16),
            pltpu.VMEM((half, total, 2 * FACTOR_FEATURES), BF16),
        ],
        compiler_params=params,
    )(me_arr, mine, recv, vertical_attend_matrix, vertical_exit_matrix, averaged_product_flanks.T)
    alignment_output = jnp.swapaxes(align, 0, 1)
    right_other = swap(right, 1)
    right_other = jnp.concatenate([right_other[:, count:], right_other[:, :count]], axis=1)

    def change_of(factor):
        outer = jnp.einsum("isc,jsd->ijcd", left, factor, preferred_element_type=F32) / total
        outer = outer.astype(BF16).reshape(own, half, FACTOR_FEATURES * FACTOR_FEATURES)
        return jnp.einsum("ijk,kz->ijz", outer, averaged_product_exit, preferred_element_type=F32)

    mine_change = change_of(right)
    other_change = change_of(right_other)
    odd = (me & 1) == 1
    even_part = jnp.where(odd, other_change, mine_change).reshape(own, slots, 1, own, channels)
    odd_part = jnp.where(odd, mine_change, other_change).reshape(own, slots, 1, own, channels)
    change = jnp.concatenate([even_part, odd_part], axis=2).reshape(own, length, channels)
    pair_output_state = (couple_tensor.astype(F32) + change).astype(BF16)
    return (alignment_output, pair_output_state)


def solution(mesh):
    devices = mesh.shape["dap"]

    def shards(homolog_tensor, couple_tensor, *rest):
        seqs, length, features = homolog_tensor.shape
        own = couple_tensor.shape[0]
        power = devices >= 8 and devices & (devices - 1) == 0
        fits = devices * seqs <= 64 and length <= 32 and features % LANES == 0
        exact = own * devices == length and (own * length) <= LANES and (length // 2) % 4 == 0
        aligned = length % 16 == 0 and (devices // 2 * seqs) % 16 == 0
        if power and fits and exact and aligned:
            return small_shards(devices, homolog_tensor, couple_tensor, *rest)
        return general_shards(homolog_tensor, couple_tensor, *rest)

    placed = (
        P(("groups", "dap"), None, None),
        P(("groups", "dap"), None, None),
        P("groups", None),
        P(),
        P(),
        P(),
        P(),
        P(),
        P(),
        P(),
    )
    return jax.shard_map(
        shards,
        mesh=mesh,
        in_specs=placed,
        out_specs=(P("groups", "dap", None), P(("groups", "dap"), None, None)),
        check_vma=False,
    )
```

```python
import functools

import jax
import jax.numpy as jnp
from jax import lax
from jax.experimental import pallas as pl
from jax.experimental.pallas import tpu as pltpu
from jax.sharding import PartitionSpec as P

HEAD_NUMBER = 8
HEAD_WIDTH = 32
FACTOR_FEATURES = 32
LANES = 128
BF16 = jnp.bfloat16
F32 = jnp.float32


def standardise_features(values):
    values = values.astype(jnp.float32)
    center = values - jnp.mean(values, axis=-1, keepdims=True)
    spread = jnp.mean(center * center, axis=-1, keepdims=True)
    return center * lax.rsqrt(spread + 1e-05)


def attend(normed, w_qkvg, w_out, bias):
    batch, length = (normed.shape[0], normed.shape[1])
    proj = jnp.einsum("blc,cf->blf", normed, w_qkvg, preferred_element_type=jnp.float32)
    proj = proj.reshape(batch, length, 4, HEAD_NUMBER, HEAD_WIDTH)
    query = (proj[:, :, 0] * HEAD_WIDTH ** (-0.5)).astype(jnp.bfloat16)
    keys = proj[:, :, 1].astype(jnp.bfloat16)
    values = proj[:, :, 2].astype(jnp.bfloat16)
    gate = proj[:, :, 3]
    if bias is None:
        bias = jnp.zeros((HEAD_NUMBER, length, length), jnp.bfloat16)

    def one_head(items):
        qh, kh, vh, bh = items
        scores = jnp.einsum("bid,bjd->bij", qh, kh, preferred_element_type=jnp.float32)
        scores = scores + bh.astype(jnp.float32)[None]
        weights = jax.nn.softmax(scores, axis=-1).astype(jnp.bfloat16)
        return jnp.einsum("bij,bjd->bid", weights, vh, preferred_element_type=jnp.float32)

    heads = lax.map(
        one_head,
        (jnp.moveaxis(query, 2, 0), jnp.moveaxis(keys, 2, 0), jnp.moveaxis(values, 2, 0), bias),
    )
    heads = jnp.moveaxis(heads, 0, 2)
    gated = (
        (jax.nn.sigmoid(gate) * heads)
        .astype(jnp.bfloat16)
        .reshape(batch, length, HEAD_NUMBER * HEAD_WIDTH)
    )
    return jnp.einsum("blk,kc->blc", gated, w_out, preferred_element_type=jnp.float32)


def general_shards(
    homolog_tensor,
    couple_tensor,
    horizontal_drop_filter,
    couple_offset_matrix,
    horizontal_attend_matrix,
    horizontal_exit_matrix,
    vertical_attend_matrix,
    vertical_exit_matrix,
    averaged_product_flanks,
    averaged_product_exit,
):
    normed_pair = standardise_features(couple_tensor).astype(jnp.bfloat16)
    own_bias = jnp.einsum(
        "ijz,zh->hij", normed_pair, couple_offset_matrix, preferred_element_type=jnp.float32
    ).astype(jnp.bfloat16)
    bias = lax.all_gather(own_bias, "dap", axis=1, tiled=True)
    starting_answer = standardise_features(homolog_tensor).astype(jnp.bfloat16)
    perform_refresh = attend(
        starting_answer, horizontal_attend_matrix, horizontal_exit_matrix, bias
    )
    homolog_later = (
        homolog_tensor.astype(jnp.float32)
        + horizontal_drop_filter.astype(jnp.float32) * (1.0 / 0.9) * perform_refresh
    ).astype(jnp.bfloat16)
    incoming_blocks = lax.all_to_all(homolog_later, "dap", split_axis=1, concat_axis=0, tiled=True)
    column_layout = jnp.swapaxes(incoming_blocks, 0, 1)
    perform_refresh = attend(
        standardise_features(column_layout).astype(jnp.bfloat16),
        vertical_attend_matrix,
        vertical_exit_matrix,
        None,
    )
    alignment_output = jnp.swapaxes(
        (column_layout.astype(jnp.float32) + perform_refresh).astype(jnp.bfloat16), 0, 1
    )
    final_result = standardise_features(alignment_output).astype(jnp.bfloat16)
    factors = jnp.einsum(
        "sic,cf->sif", final_result, averaged_product_flanks, preferred_element_type=jnp.float32
    )
    left = factors[..., :FACTOR_FEATURES].astype(jnp.bfloat16)
    right = factors[..., FACTOR_FEATURES:].astype(jnp.bfloat16)
    total = left.shape[0]
    own_rows = left.shape[1]
    whole = lax.all_gather(right, "dap", axis=1, tiled=True)
    outer = jnp.einsum("sic,sjd->ijcd", left, whole, preferred_element_type=jnp.float32) / total
    outer = outer.astype(jnp.bfloat16).reshape(
        own_rows, whole.shape[1], FACTOR_FEATURES * FACTOR_FEATURES
    )
    change = jnp.einsum(
        "ijk,kz->ijz", outer, averaged_product_exit, preferred_element_type=jnp.float32
    )
    pair_output_state = (couple_tensor.astype(jnp.float32) + change).astype(jnp.bfloat16)
    return (alignment_output, pair_output_state)


def dot(a, b, ca=1, cb=0):
    return lax.dot_general(a, b, (((ca,), (cb,)), ((), ())), preferred_element_type=F32)


def iota(shape, axis):
    return lax.broadcasted_iota(jnp.int32, shape, axis)


def slot_device(me, slot, rounds):
    out = jnp.zeros_like(slot) + me
    for bit, mask in enumerate(rounds):
        out = out ^ (((slot >> bit) & 1) * mask)
    return out


def residue_order(me, length, own):
    half = length // 2
    place = iota((length, length), 0)
    other = (place >= half).astype(jnp.int32)
    rest = place - other * half
    parity = other ^ (me & 1)
    residue = ((rest // own) * 2 + parity) * own + rest % own
    return (iota((length, length), 1) == residue).astype(F32).astype(BF16)


def softmax_attention(q, k, v, bias_t, rows, groups):
    features = q.shape[1]
    per = LANES // HEAD_WIDTH
    head_of_lane = iota((rows, LANES), 1) // HEAD_WIDTH
    masks = [head_of_lane == t for t in range(per)]
    zero = jnp.zeros((rows, LANES), BF16)
    units = [(g, part) for g in range(groups) for part in range(features // LANES)]

    def piece(x, unit):
        g, part = unit
        return x[g * rows : (g + 1) * rows, part * LANES : (part + 1) * LANES]

    scores = []
    for unit in units:
        qh = piece(q, unit)
        spread = jnp.concatenate([jnp.where(m, qh, zero) for m in masks], axis=0)
        scores.append(dot(piece(k, unit), spread, 1, 1))
    scores = jnp.concatenate(scores, axis=1)
    if bias_t is not None:
        scores = scores + jnp.concatenate([bias_t] * groups, axis=1)
    e = jnp.exp(scores - jnp.max(scores, axis=0, keepdims=True))
    w = (e * (1.0 / jnp.sum(e, axis=0, keepdims=True))).astype(BF16)
    width = per * rows
    parts = []
    for n, unit in enumerate(units):
        o = dot(w[:, n * width : (n + 1) * width], piece(v, unit), 0, 0)
        acc = o[:rows]
        for t in range(1, per):
            acc = jnp.where(masks[t], o[t * rows : (t + 1) * rows], acc)
        parts.append(acc)
    count = features // LANES
    return jnp.concatenate(
        [jnp.concatenate(parts[g * count : (g + 1) * count], axis=1) for g in range(groups)], axis=0
    )


def gated_attention(x, w_ref, wo_ref, bias_t, rows, groups):
    features = x.shape[1]
    normed = standardise_features(x).astype(BF16)
    q = (dot(normed, w_ref[:, :features]) * HEAD_WIDTH ** (-0.5)).astype(BF16)
    k = dot(normed, w_ref[:, features : 2 * features]).astype(BF16)
    v = dot(normed, w_ref[:, 2 * features : 3 * features]).astype(BF16)
    o = softmax_attention(q, k, v, bias_t, rows, groups)
    gate = dot(normed, w_ref[:, 3 * features :])
    gated = (jax.nn.sigmoid(gate) * o).astype(BF16)
    return dot(gated, wo_ref[...])


def start_kernel(own, me_ref, msa_hbm, pair_hbm, wb_hbm, out_ref, msa_ref, pair_ref, wb_ref, sems):
    copies = [
        pltpu.make_async_copy(pair_hbm, pair_ref, sems.at[0]),
        pltpu.make_async_copy(wb_hbm, wb_ref, sems.at[1]),
        pltpu.make_async_copy(msa_hbm, msa_ref, sems.at[2]),
    ]
    for copy in copies:
        copy.start()
    me = me_ref[0]
    seqs, length, features = msa_ref.shape
    order = residue_order(me, length, own)
    copies[0].wait()
    copies[1].wait()
    zn = standardise_features(pair_ref[...]).astype(BF16)
    bias = dot(wb_ref[...], zn, 1, 1)
    pad = features - bias.shape[1]
    block = jnp.concatenate([bias, jnp.zeros((bias.shape[0], pad), F32)], axis=1)
    tail = out_ref.shape[0] - seqs * length - bias.shape[0]
    block = jnp.concatenate([block, jnp.zeros((tail, features), F32)], axis=0)
    out_ref[seqs * length :, :] = block.astype(BF16)
    copies[2].wait()
    for s in range(seqs):
        out_ref[s * length : (s + 1) * length, :] = dot(order, msa_ref[s]).astype(BF16)


def row_kernel(
    rounds, seqs, own, me_ref, buf_ref, other_ref, w_ref, wo_ref, drop_ref, mine_ref, send_ref, acc_ref
):
    me = me_ref[0]
    slots = buf_ref.shape[0]
    length, features = drop_ref.shape
    half = length // 2
    order = residue_order(me, length, own)
    blocks = [buf_ref[k, seqs * length : seqs * length + HEAD_NUMBER, :LANES] for k in range(slots)]
    blocks += [other_ref[k] for k in range(slots)]
    blocks = jnp.concatenate([b.astype(F32) for b in blocks], axis=0).astype(BF16)
    shape = (2 * slots * HEAD_NUMBER, HEAD_NUMBER * length)
    row = iota(shape, 0)
    lane = iota(shape, 1)
    slot = row // HEAD_NUMBER
    cross = slot // slots
    chip = slot_device(me, slot % slots, rounds) >> 1
    base = (row % HEAD_NUMBER) * length + cross * half + chip * own
    bias_t = None
    for i in range(own):
        place = (lane == base + i).astype(F32).astype(BF16)
        part = dot(blocks, place, 0, 0)[i * length : (i + 1) * length]
        bias_t = part if bias_t is None else bias_t + part
    bias_t = dot(order, bias_t.astype(BF16))
    drop = dot(order, drop_ref[...].astype(F32).astype(BF16)) * (1.0 / 0.9)

    batch = 2 * seqs
    size = batch * length
    row = iota((size, size), 0)
    turn = (iota((size, size), 1) == (row % batch) * length + row // batch).astype(F32).astype(BF16)
    step = slots

    def body(t, carry):
        blocks = [buf_ref[step * t + u, : seqs * length, :] for u in range(step)]
        x = jnp.concatenate(blocks, axis=0).astype(F32)
        refresh = gated_attention(x, w_ref, wo_ref, bias_t, length, step * seqs)
        tiled = jnp.concatenate([drop] * (step * seqs), axis=0)
        later = (x + tiled * refresh).astype(BF16)
        for u in range(step // 2):
            turned = dot(turn, later[u * size : (u + 1) * size]).reshape(length, batch, features)
            first = (t * (step // 2) + u) * batch
            acc_ref[:, pl.ds(pl.multiple_of(first, batch), batch), :] = turned
        return carry

    lax.fori_loop(0, slots // step, body, 0, unroll=True)
    mine_ref[...] = acc_ref[:half].astype(BF16)
    send_ref[...] = acc_ref[half:].astype(BF16)


def column_kernel(
    rounds,
    seqs,
    own,
    me_ref,
    mine_ref,
    recv_ref,
    w_ref,
    wo_ref,
    flanks_ref,
    align_ref,
    left_ref,
    right_ref,
    al_ref,
    fac_ref,
):
    me = me_ref[0]
    half, count, features = mine_ref.shape
    total = 2 * count
    group = half

    def body(t, carry):
        pieces = []
        for u in range(group):
            pieces += [mine_ref[group * t + u], recv_ref[group * t + u]]
        x = jnp.concatenate(pieces, axis=0).astype(F32)
        refresh = gated_attention(x, w_ref, wo_ref, None, total, group)
        aligned = (x + refresh).astype(BF16)
        normed = standardise_features(aligned).astype(BF16)
        factors = dot(normed, flanks_ref[...], 1, 1).astype(BF16)
        for u in range(group):
            al_ref[group * t + u] = aligned[u * total : (u + 1) * total]
            fac_ref[group * t + u] = factors[u * total : (u + 1) * total]
            right_ref[group * t + u] = factors[u * total : (u + 1) * total, FACTOR_FEATURES:]
        return carry

    lax.fori_loop(0, half // group, body, 0, unroll=True)
    place = iota((total, total), 1)
    cross = place // count
    within = place % count
    device = slot_device(me, within // seqs, rounds) ^ cross
    order = (iota((total, total), 0) == device * seqs + within % seqs).astype(F32).astype(BF16)
    first = (me >> 1) * own
    for i in range(own):
        align_ref[i] = dot(order, al_ref[first + i]).astype(BF16)
        left_ref[i] = fac_ref[first + i][:, :FACTOR_FEATURES]


def small_shards(
    devices,
    homolog_tensor,
    couple_tensor,
    horizontal_drop_filter,
    couple_offset_matrix,
    horizontal_attend_matrix,
    horizontal_exit_matrix,
    vertical_attend_matrix,
    vertical_exit_matrix,
    averaged_product_flanks,
    averaged_product_exit,
):
    seqs, length, features = homolog_tensor.shape
    own = couple_tensor.shape[0]
    channels = couple_tensor.shape[2]
    half = length // 2
    slots = devices // 2
    count = slots * seqs
    total = 2 * count
    me = lax.axis_index("dap").astype(jnp.int32)
    me_arr = me.reshape(1)
    smem = pl.BlockSpec(memory_space=pltpu.SMEM)
    vmem = pl.BlockSpec(memory_space=pltpu.VMEM)
    limit = 24 * 1024 * 1024
    params = pltpu.CompilerParams(vmem_limit_bytes=limit)
    rounds = []
    mask = devices // 2
    while mask > 1:
        rounds.append(mask)
        mask //= 2

    def swap(x, by):
        return lax.ppermute(x, "dap", [(i, i ^ by) for i in range(devices)])

    height = seqs * length + 16
    hbm = pl.BlockSpec(memory_space=pltpu.HBM)

    def pinned(x):
        return pltpu.with_memory_space_constraint(x, pltpu.HBM)

    new = pl.pallas_call(
        functools.partial(start_kernel, own),
        out_shape=jax.ShapeDtypeStruct((height, features), BF16),
        in_specs=[smem, hbm, hbm, hbm],
        out_specs=vmem,
        scratch_shapes=[
            pltpu.VMEM((seqs, length, features), BF16),
            pltpu.VMEM((own * length, channels), BF16),
            pltpu.VMEM((HEAD_NUMBER, channels), BF16),
            pltpu.SemaphoreType.DMA((3,)),
        ],
        compiler_params=params,
    )(
        me_arr,
        pinned(homolog_tensor),
        pinned(couple_tensor.reshape(own * length, channels)),
        pinned(couple_offset_matrix.T),
    )
    new = new[None]
    near = [new]
    far = []
    for by in rounds[:-1]:
        got = swap(jnp.concatenate(near, axis=0), by)
        far.append(swap(new, rounds[-1]))
        near.append(got)
        new = got
    far.append(swap(new, rounds[-1]))
    buf = jnp.concatenate(near + far, axis=0)
    other = swap(buf[:, seqs * length : seqs * length + HEAD_NUMBER, :LANES], 1)
    mine, send = pl.pallas_call(
        functools.partial(row_kernel, tuple(rounds), seqs, own),
        out_shape=[jax.ShapeDtypeStruct((half, count, features), BF16)] * 2,
        in_specs=[smem] + [vmem] * 5,
        out_specs=[vmem, vmem],
        scratch_shapes=[pltpu.VMEM((length, count, features), F32)],
        compiler_params=pltpu.CompilerParams(
            vmem_limit_bytes=limit
        ),
    )(me_arr, buf, other, horizontal_attend_matrix, horizontal_exit_matrix, horizontal_drop_filter)
    recv = swap(send, 1)
    align, left, right = pl.pallas_call(
        functools.partial(column_kernel, tuple(rounds), seqs, own),
        out_shape=[
            jax.ShapeDtypeStruct((own, total, features), BF16),
            jax.ShapeDtypeStruct((own, total, FACTOR_FEATURES), BF16),
            jax.ShapeDtypeStruct((half, total, FACTOR_FEATURES), BF16),
        ],
        in_specs=[smem] + [vmem] * 5,
        out_specs=[vmem] * 3,
        scratch_shapes=[
            pltpu.VMEM((half, total, features), BF16),
            pltpu.VMEM((half, total, 2 * FACTOR_FEATURES), BF16),
        ],
        compiler_params=params,
    )(me_arr, mine, recv, vertical_attend_matrix, vertical_exit_matrix, averaged_product_flanks.T)
    alignment_output = jnp.swapaxes(align, 0, 1)
    right_other = swap(right, 1)
    right_other = jnp.concatenate([right_other[:, count:], right_other[:, :count]], axis=1)

    def change_of(factor):
        outer = jnp.einsum("isc,jsd->ijcd", left, factor, preferred_element_type=F32) / total
        outer = outer.astype(BF16).reshape(own, half, FACTOR_FEATURES * FACTOR_FEATURES)
        return jnp.einsum("ijk,kz->ijz", outer, averaged_product_exit, preferred_element_type=F32)

    mine_change = change_of(right)
    other_change = change_of(right_other)
    odd = (me & 1) == 1
    even_part = jnp.where(odd, other_change, mine_change).reshape(own, slots, 1, own, channels)
    odd_part = jnp.where(odd, mine_change, other_change).reshape(own, slots, 1, own, channels)
    change = jnp.concatenate([even_part, odd_part], axis=2).reshape(own, length, channels)
    pair_output_state = (couple_tensor.astype(F32) + change).astype(BF16)
    return (alignment_output, pair_output_state)


def solution(mesh):
    devices = mesh.shape["dap"]

    def shards(homolog_tensor, couple_tensor, *rest):
        seqs, length, features = homolog_tensor.shape
        own = couple_tensor.shape[0]
        power = devices >= 8 and devices & (devices - 1) == 0
        fits = devices * seqs <= 64 and length <= 32 and features % LANES == 0
        exact = own * devices == length and (own * length) <= LANES and (length // 2) % 4 == 0
        aligned = length % 16 == 0 and (devices // 2 * seqs) % 16 == 0
        if power and fits and exact and aligned:
            return small_shards(devices, homolog_tensor, couple_tensor, *rest)
        return general_shards(homolog_tensor, couple_tensor, *rest)

    placed = (
        P(("groups", "dap"), None, None),
        P(("groups", "dap"), None, None),
        P("groups", None),
        P(),
        P(),
        P(),
        P(),
        P(),
        P(),
        P(),
    )
    return jax.shard_map(
        shards,
        mesh=mesh,
        in_specs=placed,
        out_specs=(P("groups", "dap", None), P(("groups", "dap"), None, None)),
        check_vma=False,
    )
```

```python
import functools

import jax
import jax.numpy as jnp
from jax import lax
from jax.experimental import pallas as pl
from jax.experimental.pallas import tpu as pltpu
from jax.sharding import PartitionSpec as P

HEAD_NUMBER = 8
HEAD_WIDTH = 32
FACTOR_FEATURES = 32
LANES = 128
BF16 = jnp.bfloat16
F32 = jnp.float32


def standardise_features(values):
    values = values.astype(jnp.float32)
    center = values - jnp.mean(values, axis=-1, keepdims=True)
    spread = jnp.mean(center * center, axis=-1, keepdims=True)
    return center * lax.rsqrt(spread + 1e-05)


def attend(normed, w_qkvg, w_out, bias):
    batch, length = (normed.shape[0], normed.shape[1])
    proj = jnp.einsum("blc,cf->blf", normed, w_qkvg, preferred_element_type=jnp.float32)
    proj = proj.reshape(batch, length, 4, HEAD_NUMBER, HEAD_WIDTH)
    query = (proj[:, :, 0] * HEAD_WIDTH ** (-0.5)).astype(jnp.bfloat16)
    keys = proj[:, :, 1].astype(jnp.bfloat16)
    values = proj[:, :, 2].astype(jnp.bfloat16)
    gate = proj[:, :, 3]
    if bias is None:
        bias = jnp.zeros((HEAD_NUMBER, length, length), jnp.bfloat16)

    def one_head(items):
        qh, kh, vh, bh = items
        scores = jnp.einsum("bid,bjd->bij", qh, kh, preferred_element_type=jnp.float32)
        scores = scores + bh.astype(jnp.float32)[None]
        weights = jax.nn.softmax(scores, axis=-1).astype(jnp.bfloat16)
        return jnp.einsum("bij,bjd->bid", weights, vh, preferred_element_type=jnp.float32)

    heads = lax.map(
        one_head,
        (jnp.moveaxis(query, 2, 0), jnp.moveaxis(keys, 2, 0), jnp.moveaxis(values, 2, 0), bias),
    )
    heads = jnp.moveaxis(heads, 0, 2)
    gated = (
        (jax.nn.sigmoid(gate) * heads)
        .astype(jnp.bfloat16)
        .reshape(batch, length, HEAD_NUMBER * HEAD_WIDTH)
    )
    return jnp.einsum("blk,kc->blc", gated, w_out, preferred_element_type=jnp.float32)


def general_shards(
    homolog_tensor,
    couple_tensor,
    horizontal_drop_filter,
    couple_offset_matrix,
    horizontal_attend_matrix,
    horizontal_exit_matrix,
    vertical_attend_matrix,
    vertical_exit_matrix,
    averaged_product_flanks,
    averaged_product_exit,
):
    normed_pair = standardise_features(couple_tensor).astype(jnp.bfloat16)
    own_bias = jnp.einsum(
        "ijz,zh->hij", normed_pair, couple_offset_matrix, preferred_element_type=jnp.float32
    ).astype(jnp.bfloat16)
    bias = lax.all_gather(own_bias, "dap", axis=1, tiled=True)
    starting_answer = standardise_features(homolog_tensor).astype(jnp.bfloat16)
    perform_refresh = attend(
        starting_answer, horizontal_attend_matrix, horizontal_exit_matrix, bias
    )
    homolog_later = (
        homolog_tensor.astype(jnp.float32)
        + horizontal_drop_filter.astype(jnp.float32) * (1.0 / 0.9) * perform_refresh
    ).astype(jnp.bfloat16)
    incoming_blocks = lax.all_to_all(homolog_later, "dap", split_axis=1, concat_axis=0, tiled=True)
    column_layout = jnp.swapaxes(incoming_blocks, 0, 1)
    perform_refresh = attend(
        standardise_features(column_layout).astype(jnp.bfloat16),
        vertical_attend_matrix,
        vertical_exit_matrix,
        None,
    )
    alignment_output = jnp.swapaxes(
        (column_layout.astype(jnp.float32) + perform_refresh).astype(jnp.bfloat16), 0, 1
    )
    final_result = standardise_features(alignment_output).astype(jnp.bfloat16)
    factors = jnp.einsum(
        "sic,cf->sif", final_result, averaged_product_flanks, preferred_element_type=jnp.float32
    )
    left = factors[..., :FACTOR_FEATURES].astype(jnp.bfloat16)
    right = factors[..., FACTOR_FEATURES:].astype(jnp.bfloat16)
    total = left.shape[0]
    own_rows = left.shape[1]
    whole = lax.all_gather(right, "dap", axis=1, tiled=True)
    outer = jnp.einsum("sic,sjd->ijcd", left, whole, preferred_element_type=jnp.float32) / total
    outer = outer.astype(jnp.bfloat16).reshape(
        own_rows, whole.shape[1], FACTOR_FEATURES * FACTOR_FEATURES
    )
    change = jnp.einsum(
        "ijk,kz->ijz", outer, averaged_product_exit, preferred_element_type=jnp.float32
    )
    pair_output_state = (couple_tensor.astype(jnp.float32) + change).astype(jnp.bfloat16)
    return (alignment_output, pair_output_state)


def dot(a, b, ca=1, cb=0):
    return lax.dot_general(a, b, (((ca,), (cb,)), ((), ())), preferred_element_type=F32)


def iota(shape, axis):
    return lax.broadcasted_iota(jnp.int32, shape, axis)


def slot_mask(slot, rounds):
    return sum(mask for bit, mask in enumerate(rounds) if (slot >> bit) & 1)


def slot_device(me, slot, rounds):
    out = jnp.zeros_like(slot) + me
    for bit, mask in enumerate(rounds):
        out = out ^ (((slot >> bit) & 1) * mask)
    return out


def residue_order(me, length, own):
    half = length // 2
    place = iota((length, length), 0)
    other = (place >= half).astype(jnp.int32)
    rest = place - other * half
    parity = other ^ (me & 1)
    residue = ((rest // own) * 2 + parity) * own + rest % own
    return (iota((length, length), 1) == residue).astype(F32).astype(BF16)


def softmax_attention(q, k, v, bias_t, rows, groups):
    features = q.shape[1]
    per = LANES // HEAD_WIDTH
    head_of_lane = iota((rows, LANES), 1) // HEAD_WIDTH
    masks = [head_of_lane == t for t in range(per)]
    zero = jnp.zeros((rows, LANES), BF16)
    units = [(g, part) for g in range(groups) for part in range(features // LANES)]

    def piece(x, unit):
        g, part = unit
        return x[g * rows : (g + 1) * rows, part * LANES : (part + 1) * LANES]

    scores = []
    for unit in units:
        qh = piece(q, unit)
        spread = jnp.concatenate([jnp.where(m, qh, zero) for m in masks], axis=0)
        scores.append(dot(piece(k, unit), spread, 1, 1))
    scores = jnp.concatenate(scores, axis=1)
    if bias_t is not None:
        scores = scores + jnp.concatenate([bias_t] * groups, axis=1)
    e = jnp.exp(scores - jnp.max(scores, axis=0, keepdims=True))
    w = (e * (1.0 / jnp.sum(e, axis=0, keepdims=True))).astype(BF16)
    width = per * rows
    parts = []
    for n, unit in enumerate(units):
        o = dot(w[:, n * width : (n + 1) * width], piece(v, unit), 0, 0)
        acc = o[:rows]
        for t in range(1, per):
            acc = jnp.where(masks[t], o[t * rows : (t + 1) * rows], acc)
        parts.append(acc)
    count = features // LANES
    return jnp.concatenate(
        [jnp.concatenate(parts[g * count : (g + 1) * count], axis=1) for g in range(groups)], axis=0
    )


def gated_attention(x, w_ref, wo_ref, bias_t, rows, groups):
    features = x.shape[1]
    normed = standardise_features(x).astype(BF16)
    q = (dot(normed, w_ref[:, :features]) * HEAD_WIDTH ** (-0.5)).astype(BF16)
    k = dot(normed, w_ref[:, features : 2 * features]).astype(BF16)
    v = dot(normed, w_ref[:, 2 * features : 3 * features]).astype(BF16)
    o = softmax_attention(q, k, v, bias_t, rows, groups)
    gate = dot(normed, w_ref[:, 3 * features :])
    gated = (jax.nn.sigmoid(gate) * o).astype(BF16)
    return dot(gated, wo_ref[...])


def start_kernel(own, me_ref, msa_hbm, pair_hbm, wb_hbm, out_ref, pair_ref, msa_ref, wb_ref, sems):
    copies = [
        pltpu.make_async_copy(pair_hbm, pair_ref, sems.at[0]),
        pltpu.make_async_copy(wb_hbm, wb_ref, sems.at[1]),
        pltpu.make_async_copy(msa_hbm, msa_ref, sems.at[2]),
    ]
    for copy in copies:
        copy.start()
    me = me_ref[0]
    seqs, length, features = msa_ref.shape
    order = residue_order(me, length, own)
    copies[0].wait()
    copies[1].wait()
    zn = standardise_features(pair_ref[...]).astype(BF16)
    bias = dot(wb_ref[...], zn, 1, 1)
    pad = features - bias.shape[1]
    block = jnp.concatenate([bias, jnp.zeros((bias.shape[0], pad), F32)], axis=1)
    out_ref[seqs * length :, :] = block.astype(BF16)
    copies[2].wait()
    for s in range(seqs):
        out_ref[s * length : (s + 1) * length, :] = dot(order, msa_ref[s]).astype(BF16)


def fetch_kernel(count, *refs):
    sources, targets, sems = refs[1 : count + 1], refs[count + 1 : 2 * count + 1], refs[2 * count + 1]
    copies = [pltpu.make_async_copy(a, b, sems.at[n]) for n, (a, b) in enumerate(zip(sources, targets))]
    for copy in copies:
        copy.start()
    for copy in copies:
        copy.wait()


def row_kernel(rounds, seqs, own, me_ref, other_ref, w_ref, wo_ref, drop_ref, *refs):
    *block_refs, mine_ref, send_ref, acc_ref = refs
    me = me_ref[0]
    slots = len(block_refs)
    length, features = drop_ref.shape
    half = length // 2
    order = residue_order(me, length, own)
    blocks = [ref[seqs * length :, :LANES] for ref in block_refs]
    blocks += [other_ref[k] for k in range(slots)]
    blocks = jnp.concatenate([b.astype(F32) for b in blocks], axis=0).astype(BF16)
    shape = (2 * slots * HEAD_NUMBER, HEAD_NUMBER * length)
    row = iota(shape, 0)
    lane = iota(shape, 1)
    slot = row // HEAD_NUMBER
    cross = slot // slots
    chip = slot_device(me, slot % slots, rounds) >> 1
    base = (row % HEAD_NUMBER) * length + cross * half + chip * own
    bias_t = None
    for i in range(own):
        place = (lane == base + i).astype(F32).astype(BF16)
        part = dot(blocks, place, 0, 0)[i * length : (i + 1) * length]
        bias_t = part if bias_t is None else bias_t + part
    bias_t = dot(order, bias_t.astype(BF16))
    drop = dot(order, drop_ref[...].astype(F32).astype(BF16)) * (1.0 / 0.9)

    batch = 2 * seqs
    size = batch * length
    row = iota((size, size), 0)
    turn = (iota((size, size), 1) == (row % batch) * length + row // batch).astype(F32).astype(BF16)
    x = jnp.concatenate([ref[: seqs * length, :] for ref in block_refs], axis=0).astype(F32)
    refresh = gated_attention(x, w_ref, wo_ref, bias_t, length, slots * seqs)
    tiled = jnp.concatenate([drop] * (slots * seqs), axis=0)
    later = (x + tiled * refresh).astype(BF16)
    for u in range(slots // 2):
        turned = dot(turn, later[u * size : (u + 1) * size]).reshape(length, batch, features)
        acc_ref[:, u * batch : (u + 1) * batch, :] = turned
    mine_ref[...] = acc_ref[:half].astype(BF16)
    send_ref[...] = acc_ref[half:].astype(BF16)


def column_kernel(
    rounds, seqs, own, me_ref, mine_ref, recv_ref, w_ref, wo_ref, flanks_ref, align_ref, left_ref, right_ref, al_ref
):
    me = me_ref[0]
    half, count, features = mine_ref.shape
    total = 2 * count
    pieces = []
    for r in range(half):
        pieces += [mine_ref[r], recv_ref[r]]
    x = jnp.concatenate(pieces, axis=0).astype(F32)
    refresh = gated_attention(x, w_ref, wo_ref, None, total, half)
    aligned = (x + refresh).astype(BF16)
    normed = standardise_features(aligned).astype(BF16)
    al_ref[...] = aligned.reshape(half, total, features)
    per = LANES // FACTOR_FEATURES
    groups = half // per
    right_t = jnp.concatenate([flanks_ref[FACTOR_FEATURES:, :]] * per, axis=0)
    owner = iota((LANES, features), 0) // FACTOR_FEATURES
    right = None
    for u in range(per):
        rows = jnp.concatenate(
            [normed[(g * per + u) * total : (g * per + u + 1) * total] for g in range(groups)], axis=0
        )
        part = dot(rows, jnp.where(owner == u, right_t, jnp.zeros_like(right_t)), 1, 1)
        right = part if right is None else right + part
    right_ref[...] = right.astype(BF16).reshape(groups, total, LANES)
    place = iota((total, total), 1)
    cross = place // count
    within = place % count
    device = slot_device(me, within // seqs, rounds) ^ cross
    order = (iota((total, total), 0) == device * seqs + within % seqs).astype(F32).astype(BF16)
    first = (me >> 1) * own
    deep = FACTOR_FEATURES // per
    shape = (own * FACTOR_FEATURES, FACTOR_FEATURES)
    row = iota(shape, 0) % FACTOR_FEATURES
    deal = (iota(shape, 1) == (row % deep) * per + row // deep).astype(F32).astype(BF16)
    left_t = dot(deal, flanks_ref[:FACTOR_FEATURES, :]).astype(BF16)
    owner = iota(left_t.shape, 0) // FACTOR_FEATURES
    left = None
    for i in range(own):
        mine = al_ref[first + i]
        align_ref[i] = dot(order, mine).astype(BF16)
        part = dot(
            standardise_features(mine).astype(BF16), jnp.where(owner == i, left_t, jnp.zeros_like(left_t)), 1, 1
        )
        left = part if left is None else left + part
    left_ref[...] = left.astype(BF16)


def outer_kernel(own, me_ref, left_ref, mine_ref, other_ref, exit_ref, pair_ref, out_ref, turn_ref):
    parity = me_ref[0] & 1
    groups, total, lanes = mine_ref.shape
    per = lanes // FACTOR_FEATURES
    deep = FACTOR_FEATURES // per
    length = pair_ref.shape[0] // own
    lane_group = iota((deep, lanes), 1) // FACTOR_FEATURES
    for cross in range(2):
        for g in range(groups):
            if cross:
                right = jnp.concatenate([other_ref[g, total // 2 :, :], other_ref[g, : total // 2, :]], axis=0)
            else:
                right = mine_ref[g]
            outer = (dot(left_ref[...], right, 0, 0) / total).astype(BF16).astype(F32)
            for i in range(own):
                rows = [outer[(i * per + k) * deep : (i * per + k + 1) * deep] for k in range(per)]
                for q in range(per):
                    acc = rows[q]
                    for k in range(per):
                        if k != q:
                            moved = pltpu.roll(rows[k], ((k - q) * FACTOR_FEATURES) % lanes, 1)
                            acc = jnp.where(lane_group == k, moved, acc)
                    index = g * per + q
                    place = i * length + (index // own) * 2 * own + index % own
                    place = place + (parity ^ cross) * own
                    turn_ref[pl.ds(pl.multiple_of(place * deep, deep), deep), :] = acc
    out = pair_ref[...].astype(F32)
    for c in range(deep):
        rows = turn_ref[pl.ds(c, own * length, stride=deep), :].astype(BF16)
        out = out + dot(rows, exit_ref[c * lanes : (c + 1) * lanes, :])
    out_ref[...] = out.astype(BF16)


def small_shards(
    devices,
    homolog_tensor,
    couple_tensor,
    horizontal_drop_filter,
    couple_offset_matrix,
    horizontal_attend_matrix,
    horizontal_exit_matrix,
    vertical_attend_matrix,
    vertical_exit_matrix,
    averaged_product_flanks,
    averaged_product_exit,
):
    seqs, length, features = homolog_tensor.shape
    own = couple_tensor.shape[0]
    channels = couple_tensor.shape[2]
    half = length // 2
    slots = devices // 2
    count = slots * seqs
    total = 2 * count
    me = lax.axis_index("dap").astype(jnp.int32)
    me_arr = me.reshape(1)
    smem = pl.BlockSpec(memory_space=pltpu.SMEM)
    vmem = pl.BlockSpec(memory_space=pltpu.VMEM)
    limit = 24 * 1024 * 1024
    params = pltpu.CompilerParams(vmem_limit_bytes=limit)
    rounds = []
    mask = devices // 2
    while mask > 1:
        rounds.append(mask)
        mask //= 2

    def swap(x, by):
        return lax.ppermute(x, "dap", [(i, i ^ by) for i in range(devices)])

    height = seqs * length + HEAD_NUMBER
    hbm = pl.BlockSpec(memory_space=pltpu.HBM)

    def pinned(x):
        return pltpu.with_memory_space_constraint(x, pltpu.HBM)

    block, pair = pl.pallas_call(
        functools.partial(start_kernel, own),
        out_shape=[
            jax.ShapeDtypeStruct((height, features), BF16),
            jax.ShapeDtypeStruct((own * length, channels), BF16),
        ],
        in_specs=[smem, hbm, hbm, hbm],
        out_specs=[vmem, vmem],
        scratch_shapes=[
            pltpu.VMEM((seqs, length, features), BF16),
            pltpu.VMEM((HEAD_NUMBER, channels), BF16),
            pltpu.SemaphoreType.DMA((3,)),
        ],
        compiler_params=params,
    )(
        me_arr,
        pinned(homolog_tensor),
        pinned(couple_tensor.reshape(own * length, channels)),
        pinned(couple_offset_matrix.T),
    )
    held = {0: block}
    for depth in range(len(rounds)):
        level = [m for m in held if bin(m).count("1") == depth]
        for m in level:
            last = max([i for i, by in enumerate(rounds) if m & by], default=-1)
            for i in [last + 1, *range(len(rounds) - 1, last + 1, -1)]:
                if i < len(rounds):
                    held[m | rounds[i]] = swap(held[m], rounds[i])
    weights = [
        horizontal_drop_filter,
        horizontal_attend_matrix,
        horizontal_exit_matrix,
        vertical_attend_matrix,
        vertical_exit_matrix,
        averaged_product_flanks.T,
        averaged_product_exit,
    ]
    drop, row_in, row_out, column_in, column_out, flanks, product_exit = pl.pallas_call(
        functools.partial(fetch_kernel, len(weights)),
        out_shape=[jax.ShapeDtypeStruct(w.shape, w.dtype) for w in weights],
        in_specs=[vmem] + [hbm] * len(weights),
        out_specs=[vmem] * len(weights),
        scratch_shapes=[pltpu.SemaphoreType.DMA((len(weights),))],
        compiler_params=params,
    )(held[rounds[0]], *[pinned(w) for w in weights])
    masks = [slot_mask(slot, rounds) for slot in range(slots)]
    blocks = [held[m] for m in masks]
    other = jnp.stack([b[seqs * length :, :LANES] for b in blocks])
    other = swap(other, 1)
    mine, send = pl.pallas_call(
        functools.partial(row_kernel, tuple(rounds), seqs, own),
        out_shape=[jax.ShapeDtypeStruct((half, count, features), BF16)] * 2,
        in_specs=[smem] + [vmem] * (4 + slots),
        out_specs=[vmem, vmem],
        scratch_shapes=[pltpu.VMEM((length, count, features), F32)],
        compiler_params=pltpu.CompilerParams(
            vmem_limit_bytes=limit
        ),
    )(me_arr, other, row_in, row_out, drop, *blocks)
    recv = swap(send, 1)
    align, left, right = pl.pallas_call(
        functools.partial(column_kernel, tuple(rounds), seqs, own),
        out_shape=[
            jax.ShapeDtypeStruct((own, total, features), BF16),
            jax.ShapeDtypeStruct((total, own * FACTOR_FEATURES), BF16),
            jax.ShapeDtypeStruct((half * FACTOR_FEATURES // LANES, total, LANES), BF16),
        ],
        in_specs=[smem] + [vmem] * 5,
        out_specs=[vmem] * 3,
        scratch_shapes=[pltpu.VMEM((half, total, features), BF16)],
        compiler_params=params,
    )(me_arr, mine, recv, column_in, column_out, flanks)
    alignment_output = jnp.swapaxes(align, 0, 1)
    right_other = swap(right, 1)
    pair_output_state = pl.pallas_call(
        functools.partial(outer_kernel, own),
        out_shape=jax.ShapeDtypeStruct((own * length, channels), BF16),
        in_specs=[smem] + [vmem] * 5,
        out_specs=vmem,
        scratch_shapes=[pltpu.VMEM((own * length * FACTOR_FEATURES * FACTOR_FEATURES // LANES, LANES), F32)],
        compiler_params=params,
    )(me_arr, left, right, right_other, product_exit, pair)
    pair_output_state = pair_output_state.reshape(own, length, channels)
    return (alignment_output, pair_output_state)


def solution(mesh):
    devices = mesh.shape["dap"]

    def shards(homolog_tensor, couple_tensor, *rest):
        seqs, length, features = homolog_tensor.shape
        own = couple_tensor.shape[0]
        power = devices >= 8 and devices & (devices - 1) == 0
        fits = devices * seqs <= 64 and length <= 32 and features % LANES == 0
        exact = own * devices == length and (own * length) <= LANES and (length // 2) % 4 == 0
        exact = exact and couple_tensor.shape[2] == LANES
        aligned = length % 16 == 0 and (devices // 2 * seqs) % 16 == 0
        if power and fits and exact and aligned:
            return small_shards(devices, homolog_tensor, couple_tensor, *rest)
        return general_shards(homolog_tensor, couple_tensor, *rest)

    placed = (
        P(("groups", "dap"), None, None),
        P(("groups", "dap"), None, None),
        P("groups", None),
        P(),
        P(),
        P(),
        P(),
        P(),
        P(),
        P(),
    )
    return jax.shard_map(
        shards,
        mesh=mesh,
        in_specs=placed,
        out_specs=(P("groups", "dap", None), P(("groups", "dap"), None, None)),
        check_vma=False,
    )
```
